512 devices in a mesh: row: 128 (over z, x_hi, y), col: 4 (over x_lo, core).
Axes of the slice: x: 4 (x_hi: 2, x_lo: 2; x = x_hi * 2 + x_lo), y: 8, z: 8, core: 2. Of those that a mesh axis runs over, the one named last changes fastest.
Arguments:
- features: bfloat16 [131072, 256], P(('row', 'col')), may hold values from -6 to 6
- weight: bfloat16 [256, 256], replicated, may hold values from -0.375 to 0.375
- bias: float32 [256], replicated, may hold values from -3 to 3
- block_values: bfloat16 [128, 4, 32, 128, 128], P('row', 'col'), may hold values from -0.1875 to 0.1875
- block_target: int32 [128, 4, 32], P('row', 'col'), may hold values from 0 to 9
- block_source: int32 [128, 4, 32], P('row', 'col'), may hold values from 0 to 7
- block_count: int32 [128, 4], P('row', 'col'), may hold values from 4 to 32, as said below
- cotangent: bfloat16 [131072, 256], P(('row', 'col')), may hold values from -6 to 6
Outputs:
- output: bfloat16 [131072, 256], P(('row', 'col'))
- grad_inputs: bfloat16 [131072, 256], P(('row', 'col'))
- grad_weight: float32 [256, 256], replicated
- grad_bias: float32 [256], replicated
The draws below stay inside these ranges and needn't reach their ends.
Inputs may be any that keep to these rules, and one draw needn't show every extreme that they name: `block_count`: slots at or after a device's count hold no adjacency block; some device uses all 32 slots.
All inputs are finite; a program needn't handle non-finite values.
Results may differ from the reference program's by a relative error of at most 0.006.
Values may be sent and summed in bfloat16 or wider, within the bound.
A program may use at most 64 MiB of HBM per device.

```python
import math
import jax
import jax.numpy as jnp
from jax import lax

BLK = 128
F = 256
HALF = 2
VB = 2
NB = 32
DB = 10
SB = 8
NODES = 131072
N_ROW = 128
N_COL = 4


def draw_block_count(key, part):
    key_counts, key_choice = jax.random.split(key)
    counts_drawn = jax.random.randint(key_counts, (N_ROW, N_COL), max(NB // 8, 1), 3 * NB // 4 + 1, dtype=jnp.int32)
    chosen_device = jax.random.randint(key_choice, (), 0, N_ROW * N_COL, dtype=jnp.int32)
    flat_counts = counts_drawn.reshape(-1)
    device_ids = jnp.arange(N_ROW * N_COL, dtype=jnp.int32)
    flat_counts = jnp.where(device_ids == chosen_device, jnp.int32(NB), flat_counts)
    return flat_counts.reshape(N_ROW, N_COL).astype(jnp.int32)


def place_ends(result, stream_key, least, top_value):
    extent = result.shape
    index_at = [jax.random.randint(jax.random.fold_in(stream_key, axis), (), 0, extent[axis]) for axis in range(len(extent))]
    result = result.at[tuple(index_at)].set(least)
    longest = extent.index(max(extent))
    index_at[longest] = (index_at[longest] + 1) % extent[longest]
    return result.at[tuple(index_at)].set(top_value)


def shard_levels(key, shape, shards, least, high):
    factor_of = 1.0
    for dim, parts in shards:
        steps = jax.random.uniform(jax.random.fold_in(jax.random.fold_in(key, 6), dim), (parts,), jnp.float32, least / len(shards), high / len(shards))
        factor_of = factor_of * jnp.repeat(jnp.exp(steps), shape[dim] // parts).reshape((-1,) + (1,) * (len(shape) - 1 - dim))
    return factor_of


def normal_values(key, dims, width, most, cuts=(), held_as=jnp.bfloat16):
    factor_of = shard_levels(key, dims, cuts, -0.22, 0.18) if cuts else 1.0
    values = jax.random.normal(key, dims, jnp.float32) * width * factor_of
    return jnp.minimum(jnp.maximum(values, -most), most).astype(held_as)


def setup_inputs(seed: int = 0) -> dict:
    key_list = jax.random.split(jax.random.key(seed), 9)
    return {
        "features": normal_values(key_list[0], (NODES, F), 1.0, 6.0, ((0, 512),)),
        "weight": normal_values(key_list[1], (F, F), F ** -0.5, 0.375),
        "bias": normal_values(key_list[2], (F,), 0.5, 3.0, (), jnp.float32),
        "block_values": normal_values(key_list[3], (N_ROW, N_COL, NB, BLK, BLK), 1024 ** -0.5, 0.1875, ((0, 128), (1, 4))),
        "block_target": place_ends(jax.random.randint(key_list[4], (N_ROW, N_COL, NB), 0, DB), jax.random.fold_in(key_list[4], 1), 0, DB - 1).astype(jnp.int32),
        "block_source": place_ends(jax.random.randint(key_list[5], (N_ROW, N_COL, NB), 0, SB), jax.random.fold_in(key_list[5], 1), 0, SB - 1).astype(jnp.int32),
        "block_count": draw_block_count(jax.random.fold_in(key_list[8], 71), 0),
        "cotangent": normal_values(key_list[7], (NODES, F), 1.0, 6.0, ((0, 512),)),
    }


def silu_slope(argument):
    sigmoid_value = jax.nn.sigmoid(argument)
    return sigmoid_value * (1.0 + argument * (1.0 - sigmoid_value))

def reference(features, weight, bias, block_values, block_target, block_source, block_count, cotangent):
    span_count = 2 * HALF + 1
    dest_total = span_count * VB
    source_total = N_COL * VB
    hidden = jnp.dot(features, weight, preferred_element_type=jnp.float32).astype(jnp.bfloat16)
    hidden_blocks = hidden.reshape(N_ROW, source_total, BLK, F)
    slot_ids = jnp.arange(NB, dtype=jnp.int32)
    live_all = (slot_ids[None, None, :] < block_count[:, :, None]).astype(jnp.float32)
    dest_ids = jnp.arange(dest_total, dtype=jnp.int32)
    source_ids = jnp.arange(source_total, dtype=jnp.int32)
    row_ids = jnp.arange(N_ROW, dtype=jnp.int32)

    def forward_row(accumulated, row_index):
        row_sources = hidden_blocks[row_index]
        picked = jnp.take(row_sources, block_source[row_index], axis=0)
        products = jnp.einsum('csij,csjf->csif', block_values[row_index].astype(jnp.float32), picked.astype(jnp.float32), precision=lax.Precision.HIGHEST)
        selector = (block_target[row_index][:, None, :] == dest_ids[None, :, None]).astype(jnp.float32) * live_all[row_index][:, None, :]
        partial_value = jnp.einsum('cds,csif->cdif', selector, products, precision=lax.Precision.HIGHEST)
        partial_value = partial_value.reshape(N_COL, span_count, VB, BLK, F)
        for offset in range(span_count):
            target_row = ((row_index + offset - HALF) % N_ROW).astype(jnp.int32)
            accumulated = accumulated.at[target_row].add(partial_value[:, offset])
        return (accumulated, None)
    start_sum = jnp.zeros((N_ROW, N_COL, VB, BLK, F), jnp.float32)
    aggregate, _ = lax.scan(forward_row, start_sum, row_ids)
    aggregate = aggregate.reshape(NODES, F)
    pre_value = aggregate + bias.astype(jnp.float32)[None, :]
    output = jax.nn.silu(pre_value).astype(jnp.bfloat16)
    grad_pre_exact = cotangent.astype(jnp.float32) * silu_slope(pre_value)
    grad_pre = grad_pre_exact.astype(jnp.bfloat16)
    grad_blocks = grad_pre.reshape(N_ROW, N_COL, VB, BLK, F)

    def backward_row(unused, row_index):
        fetched = jnp.stack([grad_blocks[((row_index + offset - HALF) % N_ROW).astype(jnp.int32)] for offset in range(span_count)], axis=1)
        fetched = fetched.reshape(N_COL, dest_total, BLK, F)
        picked = jax.vmap(lambda table_rows, chosen: jnp.take(table_rows, chosen, axis=0))(fetched, block_target[row_index])
        products = jnp.einsum('csji,csjf->csif', block_values[row_index].astype(jnp.float32), picked.astype(jnp.float32), precision=lax.Precision.HIGHEST)
        selector = (block_source[row_index][:, None, :] == source_ids[None, :, None]).astype(jnp.float32) * live_all[row_index][:, None, :]
        sums = jnp.einsum('cbs,csif->bif', selector, products, precision=lax.Precision.HIGHEST)
        return (unused, sums)
    _, source_sums = lax.scan(backward_row, jnp.zeros((), jnp.float32), row_ids)
    grad_source = source_sums.reshape(NODES, F).astype(jnp.bfloat16)
    grad_inputs = lax.dot_general(grad_source, weight, (((1,), (1,)), ((), ())), preferred_element_type=jnp.float32).astype(jnp.bfloat16)
    normalizer = 1.0 / math.sqrt(NODES)
    grad_weight = jnp.dot(features.T, grad_source, preferred_element_type=jnp.float32) * normalizer
    grad_bias = lax.optimization_barrier(jnp.sum(grad_pre_exact, axis=0)) * normalizer
    return (output, grad_inputs, grad_weight, grad_bias)
```

```python
import math

import jax
import jax.numpy as jnp
from jax import lax
from jax.experimental import pallas as pl
from jax.experimental.pallas import tpu as pltpu
from jax.sharding import PartitionSpec as P

BLK = 128
HALF = 2
VB = 2
SPAN = 2 * HALF + 1
COLS = 4
ROWS = 128
NY = 8
NZ = 8
MESH = pl.DeviceIdType.MESH
F32 = jnp.float32
BF16 = jnp.bfloat16


def densify(target, source, count, values, dense, wide, first, twice):
    dense[...] = jnp.zeros_like(dense)

    @pl.loop(0, SPAN * VB * COLS * VB)
    def _(cell):
        first[cell] = -1

    @pl.loop(0, count[0, 0])
    def _(slot):
        t = target[0, 0, slot]
        e = source[0, 0, slot]
        cell = t * (COLS * VB) + e
        rows = pl.ds(pl.multiple_of(t * BLK, BLK), BLK)
        lanes = pl.ds(pl.multiple_of(e * BLK, BLK), BLK)
        held = first[cell]

        @pl.when(held < 0)
        def _():
            dense[rows, lanes] = values[0, 0, slot]
            first[cell] = slot
            twice[slot] = 0

        @pl.when(held >= 0)
        def _():
            @pl.when(twice[held] == 0)
            def _():
                wide[held] = values[0, 0, held].astype(F32)
                twice[held] = 1

            wide[held] += values[0, 0, slot].astype(F32)
            dense[rows, lanes] = wide[held].astype(BF16)


def dot(a, b):
    return jnp.dot(a, b, preferred_element_type=F32)


def split(value):
    high = value.astype(BF16)
    return high, (value - high.astype(F32)).astype(BF16)


def layer(
    x_hbm, weight, bias, adj, cot,
    out, grad_in, grad_w, grad_b,
    xg, adj_t, part, part_in, g_all, term, term_in,
    s1_out, s1_in, s2_out, s2_in, s3_buf, s4_buf, s5_buf,
    x_sem, a_send, a_recv, b_send, b_recv, c_send, c_recv, d_send, d_recv, r_send, r_recv,
):
    r = lax.axis_index("row")
    c = lax.axis_index("col")
    z = r // (2 * NY)
    xh = (r // NY) % 2
    y = r % NY
    k = xh * COLS + c
    inner = r % (2 * NY)

    def at_row(distance):
        return (lax.rem(r + distance + ROWS, ROWS), c)

    def at_col(step):
        return (r, lax.rem(c + step, COLS))

    def at_k(other):
        return (z * (2 * NY) + (other // COLS) * NY + y, lax.rem(other, COLS))

    def at_z(other):
        return (other * (2 * NY) + inner, c)

    def at_y(other):
        return (r - y + other, c)

    def ahead(me, step):
        return lax.rem(me + step, 8)

    def send(src, dst, send_sem, recv_sem, device):
        copy = pltpu.make_async_remote_copy(
            src_ref=src, dst_ref=dst, send_sem=send_sem, recv_sem=recv_sem,
            device_id=device, device_id_type=MESH,
        )
        copy.start()
        return copy

    def landed(dst, sem):
        pltpu.make_async_copy(dst, dst, sem).wait()

    own_x = pltpu.make_async_copy(x_hbm, xg.at[c], x_sem)
    own_x.start()
    barrier = pltpu.get_barrier_semaphore()
    for distance in (1, -1, 2, -2):
        pl.semaphore_signal(barrier, inc=1, device_id=at_row(distance), device_id_type=MESH)
    for step in range(1, 8):
        for device in (at_k(ahead(k, step)), at_z(ahead(z, step)), at_y(ahead(y, step))):
            pl.semaphore_signal(barrier, inc=1, device_id=device, device_id_type=MESH)
    pl.semaphore_wait(barrier, 4 + 3 * 7)

    pending = []
    for step in (2, 3, 1):
        pending.append(
            send(x_hbm, xg.at[c], a_send.at[step], a_recv.at[c], at_col(step))
        )

    for i in range(SPAN):
        for j in range(COLS):
            adj_t[j * 256:(j + 1) * 256, i * 256:(i + 1) * 256] = adj[
                i * 256:(i + 1) * 256, j * 256:(j + 1) * 256
            ].T
    own_x.wait()
    for step in (1, 2, 3):
        other = lax.rem(c + step, COLS)
        landed(xg.at[other], a_recv.at[other])

    gathered = xg[...].reshape(COLS * 256, 256)
    for offset in (0, 4, 1, 3):
        part[offset] = dot(adj[offset * 256:(offset + 1) * 256, :], gathered).astype(BF16)
        pending.append(
            send(part.at[offset], part_in.at[offset], b_send.at[offset], b_recv.at[offset], at_row(offset - HALF))
        )
    mixed = dot(adj[HALF * 256:(HALF + 1) * 256, :], gathered)
    for offset in (1, 3, 0, 4):
        landed(part_in.at[offset], b_recv.at[offset])
        mixed += part_in[offset].astype(F32)

    high, low = split(mixed)
    pre = dot(high, weight[...]) + dot(low, weight[...]) + bias[...]
    sig = 1.0 / (1.0 + jnp.exp(-pre))
    exact = cot[...].astype(F32) * (sig * (1.0 + pre * (1.0 - sig)))
    grad = exact.astype(BF16)
    g_all[HALF] = grad
    for offset in (0, 4, 1, 3):
        pending.append(
            send(g_all.at[HALF], g_all.at[offset], c_send.at[offset], c_recv.at[offset], at_row(HALF - offset))
        )
    out[...] = (pre * sig).astype(BF16)

    across = (((0,), (0,)), ((), ()))
    w_term = lax.dot_general(high, grad, across, preferred_element_type=F32) + lax.dot_general(
        low, grad, across, preferred_element_type=F32
    )
    s1_out[...] = w_term.reshape(8, 32, 256)
    for step in range(1, 8):
        other = ahead(k, step)
        pending.append(
            send(s1_out.at[other], s1_in.at[k], r_send.at[0, step], r_recv.at[0, k], at_k(other))
        )
    s1_in[k] = s1_out[k]
    b_term = jnp.sum(exact, axis=0, keepdims=True)
    b_tile = jnp.concatenate([b_term[:, :128], b_term[:, 128:], jnp.zeros((6, 128), F32)], axis=0)

    for step in range(1, 8):
        other = ahead(k, step)
        landed(s1_in.at[other], r_recv.at[0, other])
    total = s1_in[0]
    for i in range(1, 8):
        total += s1_in[i]
    for i in range(8):
        s2_out[i, 0] = total[(i // 2) * 8:(i // 2 + 1) * 8, (i % 2) * 128:(i % 2 + 1) * 128]
        s2_out[i, 1] = b_tile
    for step in range(1, 8):
        other = ahead(z, step)
        pending.append(
            send(s2_out.at[other], s2_in.at[z], r_send.at[1, step], r_recv.at[1, z], at_z(other))
        )
    s2_in[z] = s2_out[z]

    for offset in (1, 3, 0, 4):
        landed(g_all.at[offset], c_recv.at[offset])
    fetched = g_all[...].reshape(SPAN * 256, 256)
    for step in (2, 3, 1):
        other = lax.rem(c + step, COLS)
        rows = pl.ds(pl.multiple_of(other * 256, 256), 256)
        term[step] = dot(adj_t[rows, :], fetched).astype(BF16)
        pending.append(
            send(term.at[step], term_in.at[c], d_send.at[step], d_recv.at[c], at_col(step))
        )
    source = dot(adj_t[pl.ds(pl.multiple_of(c * 256, 256), 256), :], fetched)

    for step in range(1, 8):
        other = ahead(z, step)
        landed(s2_in.at[other], r_recv.at[1, other])
    total = s2_in[0]
    for i in range(1, 8):
        total += s2_in[i]
    s3_buf[y] = total
    for step in range(1, 8):
        other = ahead(y, step)
        pending.append(
            send(s3_buf.at[y], s3_buf.at[y], r_send.at[2, step], r_recv.at[2, y], at_y(other))
        )
    for step in range(1, 8):
        other = ahead(y, step)
        landed(s3_buf.at[other], r_recv.at[2, other])
    total = s3_buf[0]
    for i in range(1, 8):
        total += s3_buf[i]
    total = total * (1.0 / math.sqrt(256 * ROWS * COLS))
    s4_buf[z] = total[0]
    for step in range(1, 8):
        other = ahead(z, step)
        pending.append(
            send(s4_buf.at[z], s4_buf.at[z], r_send.at[3, step], r_recv.at[3, z], at_z(other))
        )
    s5_buf[k, 8] = total[1]

    for step in (1, 2, 3):
        other = lax.rem(c + step, COLS)
        landed(term_in.at[other], d_recv.at[other])
        source += term_in[other].astype(F32)
    grad_in[...] = lax.dot_general(
        source.astype(BF16), weight[...], (((1,), (1,)), ((), ())), preferred_element_type=F32
    ).astype(BF16)

    for step in range(1, 8):
        other = ahead(z, step)
        landed(s4_buf.at[other], r_recv.at[3, other])
    for i in range(8):
        s5_buf[k, i] = s4_buf[i]
    for step in range(1, 8):
        other = ahead(k, step)
        pending.append(
            send(s5_buf.at[k], s5_buf.at[k], r_send.at[4, step], r_recv.at[4, k], at_k(other))
        )
    for step in range(1, 8):
        other = ahead(k, step)
        landed(s5_buf.at[other], r_recv.at[4, other])
    b_sum = s5_buf[0, 8]
    for i in range(1, 8):
        b_sum += s5_buf[i, 8]
    for i in range(8):
        for j in range(8):
            grad_w[i * 32 + (j // 2) * 8:i * 32 + (j // 2 + 1) * 8, (j % 2) * 128:(j % 2 + 1) * 128] = s5_buf[i, j]
    grad_b[:, :128] = b_sum[0:1]
    grad_b[:, 128:] = b_sum[1:2]
    for copy in pending:
        copy.wait_send()


def shards(
    features, weight, bias, block_values, block_target, block_source, block_count, cotangent
):
    slots = block_values.shape[2]
    vmem = pl.BlockSpec(memory_space=pltpu.VMEM)
    smem = pl.BlockSpec(memory_space=pltpu.SMEM)
    adjacency = pl.pallas_call(
        densify,
        out_shape=jax.ShapeDtypeStruct((SPAN * VB * BLK, COLS * VB * BLK), BF16),
        in_specs=[smem, smem, smem, vmem],
        out_specs=vmem,
        scratch_shapes=[
            pltpu.VMEM((slots, BLK, BLK), F32),
            pltpu.SMEM((SPAN * VB * COLS * VB,), jnp.int32),
            pltpu.SMEM((slots,), jnp.int32),
        ],
        compiler_params=pltpu.CompilerParams(vmem_limit_bytes=16 << 20),
        name="densify",
    )(block_target, block_source, block_count, block_values)

    dma = pltpu.SemaphoreType.DMA
    output, grad_inputs, grad_weight, grad_bias = pl.pallas_call(
        layer,
        out_shape=(
            jax.ShapeDtypeStruct((256, 256), BF16),
            jax.ShapeDtypeStruct((256, 256), BF16),
            jax.ShapeDtypeStruct((256, 256), F32),
            jax.ShapeDtypeStruct((1, 256), F32),
        ),
        in_specs=[pl.BlockSpec(memory_space=pl.ANY), vmem, vmem, vmem, vmem],
        out_specs=(vmem, vmem, vmem, vmem),
        scratch_shapes=[
            pltpu.VMEM((COLS, 256, 256), BF16),
            pltpu.VMEM((COLS * 256, SPAN * 256), BF16),
            pltpu.VMEM((SPAN, 256, 256), BF16),
            pltpu.VMEM((SPAN, 256, 256), BF16),
            pltpu.VMEM((SPAN, 256, 256), BF16),
            pltpu.VMEM((COLS, 256, 256), BF16),
            pltpu.VMEM((COLS, 256, 256), BF16),
            pltpu.VMEM((8, 32, 256), F32),
            pltpu.VMEM((8, 32, 256), F32),
            pltpu.VMEM((8, 2, 8, 128), F32),
            pltpu.VMEM((8, 2, 8, 128), F32),
            pltpu.VMEM((8, 2, 8, 128), F32),
            pltpu.VMEM((8, 8, 128), F32),
            pltpu.VMEM((8, 9, 8, 128), F32),
            dma,
            dma((COLS,)),
            dma((COLS,)),
            dma((SPAN,)),
            dma((SPAN,)),
            dma((SPAN,)),
            dma((SPAN,)),
            dma((COLS,)),
            dma((COLS,)),
            dma((5, 8)),
            dma((5, 8)),
        ],
        compiler_params=pltpu.CompilerParams(
            collective_id=0, has_side_effects=True, vmem_limit_bytes=32 << 20
        ),
        name="layer",
    )(features, weight, bias.reshape(1, 256), adjacency, cotangent)
    return output, grad_inputs, grad_weight, grad_bias.reshape(256)


def solution(mesh):
    return jax.shard_map(
        shards,
        mesh=mesh,
        in_specs=(
            P(("row", "col"), None),
            P(),
            P(),
            P("row", "col", None, None, None),
            P("row", "col", None),
            P("row", "col", None),
            P("row", "col"),
            P(("row", "col"), None),
        ),
        out_specs=(P(("row", "col"), None), P(("row", "col"), None), P(), P()),
        check_vma=False,
    )
```

```python
import math

import jax
import jax.numpy as jnp
from jax import lax
from jax.experimental import pallas as pl
from jax.experimental.pallas import tpu as pltpu
from jax.sharding import PartitionSpec as P

BLK = 128
HALF = 2
VB = 2
SPAN = 2 * HALF + 1
COLS = 4
ROWS = 128
NY = 8
NZ = 8
SLOTS = 32
VMEM_BYTES = 63 << 20
CELLS = SPAN * VB * COLS * VB
MESH = pl.DeviceIdType.MESH
F32 = jnp.float32
BF16 = jnp.bfloat16


def dot(a, b):
    return jnp.dot(a, b, preferred_element_type=F32)


def split(value):
    high = value.astype(BF16)
    return high, (value - high.astype(F32)).astype(BF16)


def layer(
    x_hbm, weight_hbm, bias_hbm, values_hbm, target_hbm, source_hbm, count_hbm, cot_hbm,
    out_hbm, grad_in_hbm, grad_w_hbm, grad_b_hbm,
    out, grad_in, grad_w, grad_b, weight, bias, cot, values, target, source_of, count, table_v, table, wide, adj, fwd,
    xg, adj_t, part, part_in, g_all, term, term_in,
    w_own, w_out, w_in, w_z, w_y, w_k, bias_k, bias_z, bias_y,
    in_sem, a_send, a_recv, b_send, b_recv, c_send, c_recv, d_send, d_recv, r_send, r_recv,
):
    r = lax.axis_index("row")
    c = lax.axis_index("col")
    z = r // (2 * NY)
    xh = (r // NY) % 2
    y = r % NY
    k = xh * COLS + c
    inner = r % (2 * NY)

    def at_row(distance):
        return (lax.rem(r + distance + ROWS, ROWS), c)

    def at_col(step):
        return (r, lax.rem(c + step, COLS))

    def at_k(other):
        return (z * (2 * NY) + (other // COLS) * NY + y, lax.rem(other, COLS))

    def at_z(other):
        return (other * (2 * NY) + inner, c)

    def at_y(other):
        return (r - y + other, c)

    def ahead(me, step):
        return lax.rem(me + step, 8)

    def send(src, dst, send_sem, recv_sem, device):
        copy = pltpu.make_async_remote_copy(
            src_ref=src, dst_ref=dst, send_sem=send_sem, recv_sem=recv_sem,
            device_id=device, device_id_type=MESH,
        )
        copy.start()
        return copy

    def landed(dst, sem):
        pltpu.make_async_copy(dst, dst, sem).wait()

    def total_of(parts):
        total = parts[0].astype(F32)
        for i in range(1, 8):
            total += parts[i].astype(F32)
        return total

    def local(i, src, dst):
        copy = pltpu.make_async_copy(src, dst, in_sem.at[i])
        copy.start()
        return copy

    barrier = pltpu.get_barrier_semaphore()
    for step in range(1, 8):
        for device in (at_k(ahead(k, step)), at_z(ahead(z, step)), at_y(ahead(y, step))):
            pl.semaphore_signal(barrier, inc=1, device_id=device, device_id_type=MESH)
    for distance in (1, -1, 2, -2):
        pl.semaphore_signal(barrier, inc=1, device_id=at_row(distance), device_id_type=MESH)
    scalars = [
        local(0, target_hbm, target),
        local(1, source_hbm, source_of),
        local(2, count_hbm, count),
    ]
    own_x = local(3, x_hbm, xg.at[c])
    values_in = local(4, values_hbm, values)
    late = [local(5, weight_hbm, weight), local(6, bias_hbm, bias), local(7, cot_hbm, cot)]
    pl.semaphore_wait(barrier, 4 + 3 * 7)
    pending = []
    sibling = c + 1 - 2 * lax.rem(c, 2)
    facing = lax.rem(c + 2, COLS)
    behind = lax.rem(sibling + 2, COLS)
    halves = (pl.ds(0, 128), pl.ds(128, 128))
    for i, rows in enumerate(halves):
        pending.append(
            send(x_hbm.at[rows], xg.at[c, rows], a_send.at[i], a_recv.at[i], (r, facing))
        )
    pending.append(send(x_hbm, xg.at[c], a_send.at[2], a_recv.at[2], (r, sibling)))
    for copy in scalars:
        copy.wait()
    lane = lax.broadcasted_iota(jnp.int32, (SLOTS, 128), 1)
    sub = lax.broadcasted_iota(jnp.int32, (SLOTS, 128), 0)
    in_row = jnp.full((SLOTS, 128), CELLS, jnp.int32)
    in_col = jnp.full((SLOTS, 128), CELLS, jnp.int32)
    for slot in range(SLOTS):
        cell = jnp.where(
            slot < count[0, 0], target[0, 0, slot] * (COLS * VB) + source_of[0, 0, slot], CELLS
        )
        in_row = jnp.where(lane == slot, cell, in_row)
        in_col = jnp.where(sub == slot, cell, in_col)
    table_v[0:1, :] = jnp.min(jnp.where(in_col == lane, sub, SLOTS), axis=0, keepdims=True)
    table_v[1:2, :] = jnp.min(
        jnp.where((in_col == in_row) & (sub > lane), sub, SLOTS), axis=0, keepdims=True
    )
    tabled = local(8, table_v, table)
    tabled.wait()
    values_in.wait()
    wide[SLOTS] = jnp.zeros((BLK, BLK), F32)
    for slot in range(SLOTS - 1, -1, -1):
        wide[slot] = values[0, 0, slot].astype(F32) + wide[table[1, slot]]
    for d in range(SPAN * VB):
        for e in range(COLS * VB):
            block = wide[table[0, d * (COLS * VB) + e]].astype(BF16)
            adj[d * BLK:(d + 1) * BLK, e * BLK:(e + 1) * BLK] = block
            adj_t[e * BLK:(e + 1) * BLK, d * BLK:(d + 1) * BLK] = block.T
    for i, rows in enumerate(halves):
        landed(xg.at[facing, rows], a_recv.at[i])
        pending.append(
            send(xg.at[facing, rows], xg.at[facing, rows], a_send.at[3 + i], a_recv.at[3 + i], (r, sibling))
        )
    own_x.wait()
    landed(xg.at[sibling], a_recv.at[2])
    for copy in late:
        copy.wait()
    chip = c // 2
    near = xg[pl.ds(2 * chip, 2)].reshape(512, 256)
    near_lanes = pl.ds(pl.multiple_of(chip * 512, 512), 512)
    for offset in (0, 4, 1, 3, 2):
        fwd[offset] = dot(adj[offset * 256:(offset + 1) * 256, near_lanes], near)
    for i, rows in enumerate(halves):
        landed(xg.at[behind, rows], a_recv.at[3 + i])
    far = xg[pl.ds(2 - 2 * chip, 2)].reshape(512, 256)
    far_lanes = pl.ds(pl.multiple_of(512 - chip * 512, 512), 512)
    for offset in (0, 4, 1, 3):
        part[offset] = (
            fwd[offset] + dot(adj[offset * 256:(offset + 1) * 256, far_lanes], far)
        ).astype(BF16)
        pending.append(
            send(part.at[offset], part_in.at[offset], b_send.at[offset], b_recv.at[offset], at_row(offset - HALF))
        )
    mixed = fwd[HALF] + dot(adj[HALF * 256:(HALF + 1) * 256, far_lanes], far)
    for offset in (1, 3, 0, 4):
        landed(part_in.at[offset], b_recv.at[offset])
        mixed += part_in[offset].astype(F32)

    high, low = split(mixed)
    pre = dot(high, weight[...]) + dot(low, weight[...]) + bias[...]
    sig = 1.0 / (1.0 + jnp.exp(-pre))
    exact = cot[...].astype(F32) * (sig * (1.0 + pre * (1.0 - sig)))
    grad = exact.astype(BF16)
    g_all[HALF] = grad
    for offset in (0, 4, 1, 3):
        pending.append(
            send(g_all.at[HALF], g_all.at[offset], c_send.at[offset], c_recv.at[offset], at_row(HALF - offset))
        )
    out[...] = (pre * sig).astype(BF16)

    written = [local(9, out, out_hbm)]
    across = (((0,), (0,)), ((), ()))
    w_term = lax.dot_general(high, grad, across, preferred_element_type=F32) + lax.dot_general(
        low, grad, across, preferred_element_type=F32
    )
    w_own[...] = w_term.reshape(8, 32, 256)
    w_out[...] = w_term.reshape(8, 32, 256).astype(BF16)
    bias_k[k] = jnp.sum(exact, axis=0, keepdims=True)
    for step in range(1, 8):
        other = ahead(k, step)
        pending.append(
            send(w_out.at[other], w_in.at[k], r_send.at[0, step], r_recv.at[0, k], at_k(other))
        )
        pending.append(
            send(bias_k.at[k], bias_k.at[k], r_send.at[1, step], r_recv.at[1, k], at_k(other))
        )
    w_in[k] = jnp.zeros((32, 256), BF16)
    for step in range(1, 8):
        other = ahead(k, step)
        landed(w_in.at[other], r_recv.at[0, other])
        landed(bias_k.at[other], r_recv.at[1, other])
    w_z[z] = (w_own[k] + total_of(w_in)).astype(BF16)
    bias_z[z] = total_of(bias_k)
    for step in range(1, 8):
        other = ahead(z, step)
        pending.append(
            send(w_z.at[z], w_z.at[z], r_send.at[2, step], r_recv.at[2, z], at_z(other))
        )
        pending.append(
            send(bias_z.at[z], bias_z.at[z], r_send.at[3, step], r_recv.at[3, z], at_z(other))
        )
    for step in range(1, 8):
        other = ahead(z, step)
        landed(w_z.at[other], r_recv.at[2, other])
        landed(bias_z.at[other], r_recv.at[3, other])
    w_y[y] = total_of(w_z).astype(BF16)
    bias_y[y] = total_of(bias_z)
    for step in range(1, 8):
        other = ahead(y, step)
        pending.append(
            send(w_y.at[y], w_y.at[y], r_send.at[4, step], r_recv.at[4, y], at_y(other))
        )
        pending.append(
            send(bias_y.at[y], bias_y.at[y], r_send.at[5, step], r_recv.at[5, y], at_y(other))
        )
    for offset in (1, 3, 0, 4):
        landed(g_all.at[offset], c_recv.at[offset])
    fetched = g_all[...].reshape(SPAN * 256, 256)
    for step in (2, 3, 1):
        other = lax.rem(c + step, COLS)
        rows = pl.ds(pl.multiple_of(other * 256, 256), 256)
        term[step] = dot(adj_t[rows, :], fetched).astype(BF16)
        pending.append(
            send(term.at[step], term_in.at[c], d_send.at[step], d_recv.at[c], at_col(step))
        )
    source = dot(adj_t[pl.ds(pl.multiple_of(c * 256, 256), 256), :], fetched)
    for step in range(1, 8):
        other = ahead(y, step)
        landed(w_y.at[other], r_recv.at[4, other])
        landed(bias_y.at[other], r_recv.at[5, other])
    normalizer = 1.0 / math.sqrt(256 * ROWS * COLS)
    w_k[k] = (total_of(w_y) * normalizer).astype(BF16)
    for step in range(1, 8):
        other = ahead(k, step)
        pending.append(
            send(w_k.at[k], w_k.at[k], r_send.at[6, step], r_recv.at[6, k], at_k(other))
        )
    grad_b[...] = total_of(bias_y) * normalizer
    written.append(local(10, grad_b, grad_b_hbm))
    for step in (1, 2, 3):
        other = lax.rem(c + step, COLS)
        landed(term_in.at[other], d_recv.at[other])
        source += term_in[other].astype(F32)
    grad_in[...] = lax.dot_general(
        source.astype(BF16), weight[...], (((1,), (1,)), ((), ())), preferred_element_type=F32
    ).astype(BF16)
    written.append(local(11, grad_in, grad_in_hbm))
    for step in range(1, 8):
        other = ahead(k, step)
        landed(w_k.at[other], r_recv.at[6, other])
    grad_w[...] = w_k[...].astype(F32).reshape(256, 256)
    written.append(local(12, grad_w, grad_w_hbm))
    for copy in pending:
        copy.wait_send()
    for copy in written:
        copy.wait()


def hand_over(*refs):
    sems = refs[-1]
    n = (len(refs) - 1) // 3
    for i in range(n):
        pltpu.make_async_copy(refs[i], refs[2 * n + i], sems.at[0, i]).start()
    for i in range(n):
        pltpu.make_async_copy(refs[i], refs[2 * n + i], sems.at[0, i]).wait()
        pltpu.make_async_copy(refs[2 * n + i], refs[n + i], sems.at[1, i]).start()
    for i in range(n):
        pltpu.make_async_copy(refs[2 * n + i], refs[n + i], sems.at[1, i]).wait()


def shards(
    features, weight, bias, block_values, block_target, block_source, block_count, cotangent
):
    hbm = pl.BlockSpec(memory_space=pltpu.HBM)
    dma = pltpu.SemaphoreType.DMA
    shapes = (
        jax.ShapeDtypeStruct((256, 256), BF16),
        jax.ShapeDtypeStruct((256, 256), BF16),
        jax.ShapeDtypeStruct((256, 256), F32),
        jax.ShapeDtypeStruct((1, 256), F32),
    )
    staged = [pltpu.VMEM(leaf.shape, leaf.dtype) for leaf in shapes]
    results = pl.pallas_call(
        layer,
        out_shape=shapes,
        in_specs=[hbm] * 8,
        out_specs=(hbm,) * 4,
        scratch_shapes=[
            *staged,
            pltpu.VMEM((256, 256), BF16),
            pltpu.VMEM((1, 256), F32),
            pltpu.VMEM((256, 256), BF16),
            pltpu.VMEM((1, 1, SLOTS, BLK, BLK), BF16),
            pltpu.SMEM((1, 1, SLOTS), jnp.int32),
            pltpu.SMEM((1, 1, SLOTS), jnp.int32),
            pltpu.SMEM((1, 1), jnp.int32),
            pltpu.VMEM((2, 128), jnp.int32),
            pltpu.SMEM((2, 128), jnp.int32),
            pltpu.VMEM((SLOTS + 1, BLK, BLK), F32),
            pltpu.VMEM((SPAN * 256, COLS * 256), BF16),
            pltpu.VMEM((SPAN, 256, 256), F32),
            pltpu.VMEM((COLS, 256, 256), BF16),
            pltpu.VMEM((COLS * 256, SPAN * 256), BF16),
            pltpu.VMEM((SPAN, 256, 256), BF16),
            pltpu.VMEM((SPAN, 256, 256), BF16),
            pltpu.VMEM((SPAN, 256, 256), BF16),
            pltpu.VMEM((COLS, 256, 256), BF16),
            pltpu.VMEM((COLS, 256, 256), BF16),
            pltpu.VMEM((8, 32, 256), F32),
            pltpu.VMEM((8, 32, 256), BF16),
            pltpu.VMEM((8, 32, 256), BF16),
            pltpu.VMEM((8, 32, 256), BF16),
            pltpu.VMEM((8, 32, 256), BF16),
            pltpu.VMEM((8, 32, 256), BF16),
            pltpu.VMEM((8, 1, 256), F32),
            pltpu.VMEM((8, 1, 256), F32),
            pltpu.VMEM((8, 1, 256), F32),
            dma((13,)),
            dma((5,)),
            dma((5,)),
            dma((SPAN,)),
            dma((SPAN,)),
            dma((SPAN,)),
            dma((SPAN,)),
            dma((COLS,)),
            dma((COLS,)),
            dma((7, 8)),
            dma((7, 8)),
        ],
        compiler_params=pltpu.CompilerParams(
            collective_id=0, has_side_effects=True, vmem_limit_bytes=VMEM_BYTES
        ),
        name="layer",
    )(
        features, weight, bias.reshape(1, 256), block_values, block_target, block_source, block_count, cotangent
    )
    output, grad_inputs, grad_weight, grad_bias = pl.pallas_call(
        hand_over,
        out_shape=shapes,
        in_specs=[hbm] * 4,
        out_specs=(hbm,) * 4,
        scratch_shapes=[*staged, dma((2, 4))],
        compiler_params=pltpu.CompilerParams(vmem_limit_bytes=VMEM_BYTES),
        name="hand_over",
    )(*results)
    return output, grad_inputs, grad_weight, grad_bias.reshape(256)


def solution(mesh):
    return jax.shard_map(
        shards,
        mesh=mesh,
        in_specs=(
            P(("row", "col"), None),
            P(),
            P(),
            P("row", "col", None, None, None),
            P("row", "col", None),
            P("row", "col", None),
            P("row", "col"),
            P(("row", "col"), None),
        ),
        out_specs=(P(("row", "col"), None), P(("row", "col"), None), P(), P()),
        check_vma=False,
    )
```

```python
import math

import jax
import jax.numpy as jnp
from jax import lax
from jax.experimental import pallas as pl
from jax.experimental.pallas import tpu as pltpu
from jax.sharding import PartitionSpec as P

BLK = 128
HALF = 2
VB = 2
SPAN = 2 * HALF + 1
COLS = 4
ROWS = 128
NY = 8
NZ = 8
SLOTS = 32
VMEM_BYTES = 54810 << 10
CELLS = SPAN * VB * COLS * VB
MESH = pl.DeviceIdType.MESH
F32 = jnp.float32
BF16 = jnp.bfloat16


def dot(a, b):
    return jnp.dot(a, b, preferred_element_type=F32)


def split(value):
    high = value.astype(BF16)
    return high, (value - high.astype(F32)).astype(BF16)


def layer(
    x_hbm, weight_hbm, bias_hbm, values_hbm, target_hbm, source_hbm, count_hbm, cot_hbm,
    out, grad_in, grad_w, grad_b,
    weight, bias, cot, values, target, source_of, count, table_v, table, wide, adj, fwd, bwd,
    xg, adj_t, part, part_in, g_all, term, term_in,
    w_own, w_out, w_in, w_z, w_y, w_k, bias_k, bias_z, bias_y,
    in_sem, a_send, a_recv, b_send, b_recv, c_send, c_recv, d_send, d_recv, r_send, r_recv,
):
    r = lax.axis_index("row")
    c = lax.axis_index("col")
    z = r // (2 * NY)
    xh = (r // NY) % 2
    y = r % NY
    k = xh * COLS + c
    inner = r % (2 * NY)

    def at_row(distance):
        return (lax.rem(r + distance + ROWS, ROWS), c)

    def at_col(step):
        return (r, lax.rem(c + step, COLS))

    def at_k(other):
        return (z * (2 * NY) + (other // COLS) * NY + y, lax.rem(other, COLS))

    def at_z(other):
        return (other * (2 * NY) + inner, c)

    def at_y(other):
        return (r - y + other, c)

    def ahead(me, step):
        return lax.rem(me + step, 8)

    def send(src, dst, send_sem, recv_sem, device):
        copy = pltpu.make_async_remote_copy(
            src_ref=src, dst_ref=dst, send_sem=send_sem, recv_sem=recv_sem,
            device_id=device, device_id_type=MESH,
        )
        copy.start()

    def landed(dst, sem):
        pltpu.make_async_copy(dst, dst, sem).wait()

    def total_of(parts):
        total = parts[0].astype(F32)
        for i in range(1, 8):
            total += parts[i].astype(F32)
        return total

    def local(i, src, dst):
        copy = pltpu.make_async_copy(src, dst, in_sem.at[i])
        copy.start()
        return copy

    barrier = pltpu.get_barrier_semaphore()
    for step in range(1, 8):
        for device in (at_k(ahead(k, step)), at_z(ahead(z, step)), at_y(ahead(y, step))):
            pl.semaphore_signal(barrier, inc=1, device_id=device, device_id_type=MESH)
    for distance in (1, -1, 2, -2):
        pl.semaphore_signal(barrier, inc=1, device_id=at_row(distance), device_id_type=MESH)
    scalars = [
        local(0, target_hbm, target),
        local(1, source_hbm, source_of),
        local(2, count_hbm, count),
    ]
    own_x = local(3, x_hbm, xg.at[c])
    values_in = local(4, values_hbm, values)
    late = [local(5, weight_hbm, weight), local(6, bias_hbm, bias), local(7, cot_hbm, cot)]
    pl.semaphore_wait(barrier, 4 + 3 * 7)
    sibling = c + 1 - 2 * lax.rem(c, 2)
    facing = lax.rem(c + 2, COLS)
    behind = lax.rem(sibling + 2, COLS)
    pieces = [pl.ds(64 * i, 64) for i in range(4)]
    for i, rows in enumerate(pieces):
        send(x_hbm.at[rows], xg.at[c, rows], a_send, a_recv.at[i], (r, facing)
        )
    send(x_hbm, xg.at[c], a_send, a_recv.at[4], (r, sibling))
    for copy in scalars:
        copy.wait()
    lane = lax.broadcasted_iota(jnp.int32, (SLOTS, 128), 1)
    sub = lax.broadcasted_iota(jnp.int32, (SLOTS, 128), 0)
    in_row = jnp.full((SLOTS, 128), CELLS, jnp.int32)
    in_col = jnp.full((SLOTS, 128), CELLS, jnp.int32)
    for slot in range(SLOTS):
        cell = jnp.where(
            slot < count[0, 0], target[0, 0, slot] * (COLS * VB) + source_of[0, 0, slot], CELLS
        )
        in_row = jnp.where(lane == slot, cell, in_row)
        in_col = jnp.where(sub == slot, cell, in_col)
    table_v[0:1, :] = jnp.min(jnp.where(in_col == lane, sub, SLOTS), axis=0, keepdims=True)
    table_v[1:2, :] = jnp.min(
        jnp.where((in_col == in_row) & (sub > lane), sub, SLOTS), axis=0, keepdims=True
    )
    tabled = local(8, table_v, table)
    tabled.wait()
    values_in.wait()
    wide[SLOTS] = jnp.zeros((BLK, BLK), F32)
    for slot in range(SLOTS - 1, -1, -1):
        wide[slot] = values[0, 0, slot].astype(F32) + wide[table[1, slot]]
    for d in range(SPAN * VB):
        for e in range(COLS * VB):
            block = wide[table[0, d * (COLS * VB) + e]].astype(BF16)
            adj[d * BLK:(d + 1) * BLK, e * BLK:(e + 1) * BLK] = block
            adj_t[e * BLK:(e + 1) * BLK, d * BLK:(d + 1) * BLK] = block.T
    for i, rows in enumerate(pieces):
        landed(xg.at[facing, rows], a_recv.at[i])
        send(xg.at[facing, rows], xg.at[facing, rows], a_send, a_recv.at[5], (r, sibling)
        )
    own_x.wait()
    landed(xg.at[sibling], a_recv.at[4])
    for copy in late:
        copy.wait()
    chip = c // 2
    near_lanes = pl.ds(pl.multiple_of(chip * 512, 512), 512)

    def row_block(i):
        return pl.ds(pl.multiple_of(i * 256, 256), 256)

    near = xg[pl.ds(2 * chip, 2)].reshape(512, 256)
    for offset in range(SPAN):
        fwd[offset] = dot(adj[offset * 256:(offset + 1) * 256, near_lanes], near)
    landed(xg.at[behind], a_recv.at[5])
    far_lanes = pl.ds(pl.multiple_of(512 - chip * 512, 512), 512)
    first, second = jnp.where(y < NY // 2, 0, 4), jnp.where(y < NY // 2, 1, 3)

    def mixed_at(offset):
        return fwd[offset] + dot(adj[row_block(offset), far_lanes], xg[pl.ds(2 - 2 * chip, 2)].reshape(512, 256))

    @pl.loop(0, 4)
    def _(i):
        offset = jnp.where(i == 0, first, jnp.where(i == 1, second, jnp.where(i == 2, 4 - first, 4 - second)))
        part[offset] = mixed_at(offset).astype(BF16)
        send(part.at[offset], part_in.at[offset], b_send, b_recv, at_row(offset - HALF))

    mixed = mixed_at(HALF)
    landed(part_in.at[pl.ds(0, 4)], b_recv)
    for offset in (1, 3, 0, 4):
        mixed += part_in[offset].astype(F32)

    high, low = split(mixed)
    pre = dot(high, weight[...]) + dot(low, weight[...]) + bias[...]
    sig = 1.0 / (1.0 + jnp.exp(-pre))
    exact = cot[...].astype(F32) * (sig * (1.0 + pre * (1.0 - sig)))
    grad = exact.astype(BF16)
    g_all[HALF] = grad
    def send_grad(src, dst, distance, arrived):
        send(g_all.at[src], g_all.at[dst], c_send, c_recv.at[arrived], at_row(distance)
        )


    across = (((0,), (0,)), ((), ()))
    w_term = lax.dot_general(high, grad, across, preferred_element_type=F32) + lax.dot_general(
        low, grad, across, preferred_element_type=F32
    )
    w_own[...] = w_term.reshape(8, 32, 256)
    w_out[...] = w_term.reshape(8, 32, 256).astype(BF16)
    bias_k[k] = jnp.sum(exact, axis=0, keepdims=True)
    for step in range(1, 8):
        other = ahead(k, step)
        send(w_out.at[other], w_in.at[k], r_send.at[0], r_recv.at[0], at_k(other)
        )
        send(bias_k.at[k], bias_k.at[k], r_send.at[1], r_recv.at[1], at_k(other)
        )
    send_grad(HALF, 1, 1, 0)
    send_grad(HALF, 3, -1, 1)
    w_in[k] = jnp.zeros((32, 256), BF16)
    out[...] = (pre * sig).astype(BF16)
    landed(w_in.at[pl.ds(0, 7)], r_recv.at[0])
    landed(bias_k.at[pl.ds(0, 7)], r_recv.at[1])
    w_y[y] = (w_own[k] + total_of(w_in)).astype(BF16)
    bias_y[y] = total_of(bias_k)
    for step in range(1, 8):
        other = ahead(y, step)
        send(w_y.at[y], w_y.at[y], r_send.at[2], r_recv.at[2], at_y(other)
        )
        send(bias_y.at[y], bias_y.at[y], r_send.at[3], r_recv.at[3], at_y(other)
        )
    landed(g_all.at[1], c_recv.at[0])
    send_grad(1, 0, 1, 2)
    landed(g_all.at[3], c_recv.at[1])
    send_grad(3, 4, -1, 2)
    close = g_all[pl.ds(1, 3)].reshape(768, 256)
    for j in range(COLS):
        bwd[j] = dot(adj_t[j * 256:(j + 1) * 256, 256:1024], close)
    landed(w_y.at[pl.ds(0, 7)], r_recv.at[2])
    landed(bias_y.at[pl.ds(0, 7)], r_recv.at[3])
    w_z[z] = total_of(w_y).astype(BF16)
    bias_z[z] = total_of(bias_y)
    for step in range(1, 8):
        other = ahead(z, step)
        send(w_z.at[z], w_z.at[z], r_send.at[4], r_recv.at[4], at_z(other)
        )
        send(bias_z.at[z], bias_z.at[z], r_send.at[5], r_recv.at[5], at_z(other)
        )
    landed(g_all.at[pl.ds(0, 2)], c_recv.at[2])

    def finished(j):
        rows = row_block(j)
        return bwd[j] + dot(adj_t[rows, 0:256], g_all[0]) + dot(adj_t[rows, 1024:1280], g_all[4])

    @pl.loop(0, 3)
    def _(i):
        step = jnp.where(i == 0, 2, jnp.where(i == 1, 3, 1))
        other = lax.rem(c + step, COLS)
        term[step] = finished(other).astype(BF16)
        send(term.at[step], term_in.at[c], d_send, d_recv, at_col(step))

    source = finished(c)
    landed(w_z.at[pl.ds(0, 7)], r_recv.at[4])
    landed(bias_z.at[pl.ds(0, 7)], r_recv.at[5])
    normalizer = 1.0 / math.sqrt(256 * ROWS * COLS)
    w_k[k] = (total_of(w_z) * normalizer).astype(BF16)
    for step in range(1, 8):
        other = ahead(k, step)
        send(w_k.at[k], w_k.at[k], r_send.at[6], r_recv.at[6], at_k(other)
        )
    grad_b[...] = total_of(bias_z) * normalizer
    landed(term_in.at[pl.ds(0, 3)], d_recv)
    for step in (1, 2, 3):
        other = lax.rem(c + step, COLS)
        source += term_in[other].astype(F32)
    grad_in[...] = lax.dot_general(
        source.astype(BF16), weight[...], (((1,), (1,)), ((), ())), preferred_element_type=F32
    ).astype(BF16)
    landed(w_k.at[pl.ds(0, 7)], r_recv.at[6])
    grad_w[...] = w_k[...].reshape(256, 256)
    landed(xg.at[pl.ds(0, 3)], a_send)
    landed(part.at[pl.ds(0, 4)], b_send)
    landed(g_all.at[pl.ds(0, 4)], c_send)
    landed(term.at[pl.ds(0, 3)], d_send)
    for i, sent in enumerate((w_out, bias_k, w_y, bias_y, w_z, bias_z, w_k)):
        landed(sent.at[pl.ds(0, 7)], r_send.at[i])


def hand_over(out, grad_in, grad_w, grad_b, out_hbm, grad_in_hbm, grad_w_hbm, grad_b_hbm, wide_w, sems):
    copies = [
        pltpu.make_async_copy(src, dst, sems.at[i])
        for i, (src, dst) in enumerate(
            ((out, out_hbm), (grad_in, grad_in_hbm), (grad_b, grad_b_hbm), (wide_w, grad_w_hbm))
        )
    ]
    for copy in copies[:3]:
        copy.start()
    wide_w[...] = grad_w[...].astype(F32)
    copies[3].start()
    for copy in copies:
        copy.wait()


def shards(
    features, weight, bias, block_values, block_target, block_source, block_count, cotangent
):
    vmem = pl.BlockSpec(memory_space=pltpu.VMEM)
    hbm = pl.BlockSpec(memory_space=pltpu.HBM)
    dma = pltpu.SemaphoreType.DMA
    shapes = [
        jax.ShapeDtypeStruct((256, 256), BF16),
        jax.ShapeDtypeStruct((256, 256), BF16),
        jax.ShapeDtypeStruct((256, 256), BF16),
        jax.ShapeDtypeStruct((1, 256), F32),
    ]
    results = pl.pallas_call(
        layer,
        out_shape=shapes,
        in_specs=[hbm] * 8,
        out_specs=(vmem,) * 4,
        scratch_shapes=[
            pltpu.VMEM((256, 256), BF16),
            pltpu.VMEM((1, 256), F32),
            pltpu.VMEM((256, 256), BF16),
            pltpu.VMEM((1, 1, SLOTS, BLK, BLK), BF16),
            pltpu.SMEM((1, 1, SLOTS), jnp.int32),
            pltpu.SMEM((1, 1, SLOTS), jnp.int32),
            pltpu.SMEM((1, 1), jnp.int32),
            pltpu.VMEM((2, 128), jnp.int32),
            pltpu.SMEM((2, 128), jnp.int32),
            pltpu.VMEM((SLOTS + 1, BLK, BLK), F32),
            pltpu.VMEM((SPAN * 256, COLS * 256), BF16),
            pltpu.VMEM((SPAN, 256, 256), F32),
            pltpu.VMEM((COLS, 256, 256), F32),
            pltpu.VMEM((COLS, 256, 256), BF16),
            pltpu.VMEM((COLS * 256, SPAN * 256), BF16),
            pltpu.VMEM((SPAN, 256, 256), BF16),
            pltpu.VMEM((SPAN, 256, 256), BF16),
            pltpu.VMEM((SPAN, 256, 256), BF16),
            pltpu.VMEM((COLS, 256, 256), BF16),
            pltpu.VMEM((COLS, 256, 256), BF16),
            pltpu.VMEM((8, 32, 256), F32),
            pltpu.VMEM((8, 32, 256), BF16),
            pltpu.VMEM((8, 32, 256), BF16),
            pltpu.VMEM((8, 32, 256), BF16),
            pltpu.VMEM((8, 32, 256), BF16),
            pltpu.VMEM((8, 32, 256), BF16),
            pltpu.VMEM((8, 1, 256), F32),
            pltpu.VMEM((8, 1, 256), F32),
            pltpu.VMEM((8, 1, 256), F32),
            dma((9,)),
            dma,
            dma((6,)),
            dma,
            dma,
            dma,
            dma((3,)),
            dma,
            dma,
            dma((7,)),
            dma((7,)),
        ],
        compiler_params=pltpu.CompilerParams(
            collective_id=0, has_side_effects=True, vmem_limit_bytes=VMEM_BYTES
        ),
        name="layer",
    )(
        features, weight, bias.reshape(1, 256), block_values, block_target, block_source, block_count, cotangent
    )
    output, grad_inputs, grad_weight, grad_bias = pl.pallas_call(
        hand_over,
        out_shape=[*shapes[:2], jax.ShapeDtypeStruct((256, 256), F32), shapes[3]],
        in_specs=[vmem] * 4,
        out_specs=(hbm,) * 4,
        scratch_shapes=[pltpu.VMEM((256, 256), F32), dma((4,))],
        compiler_params=pltpu.CompilerParams(vmem_limit_bytes=1 << 20),
        name="hand_over",
    )(*results)
    return output, grad_inputs, grad_weight, grad_bias.reshape(256)


def solution(mesh):
    return jax.shard_map(
        shards,
        mesh=mesh,
        in_specs=(
            P(("row", "col"), None),
            P(),
            P(),
            P("row", "col", None, None, None),
            P("row", "col", None),
            P("row", "col", None),
            P("row", "col"),
            P(("row", "col"), None),
        ),
        out_specs=(P(("row", "col"), None), P(("row", "col"), None), P(), P()),
        check_vma=False,
    )
```

```python
import math

import jax
import jax.numpy as jnp
from jax import lax
from jax.experimental import pallas as pl
from jax.experimental.pallas import tpu as pltpu
from jax.sharding import PartitionSpec as P

BLK = 128
HALF = 2
VB = 2
SPAN = 2 * HALF + 1
COLS = 4
ROWS = 128
NY = 8
NZ = 8
SLOTS = 32
VMEM_BYTES = 54810 << 10
CELLS = SPAN * VB * COLS * VB
MESH = pl.DeviceIdType.MESH
F32 = jnp.float32
BF16 = jnp.bfloat16


def dot(a, b):
    return jnp.dot(a, b, preferred_element_type=F32)


def split(value):
    high = value.astype(BF16)
    return high, (value - high.astype(F32)).astype(BF16)


def layer(
    x_hbm, weight_hbm, bias_hbm, values_hbm, target_hbm, source_hbm, count_hbm, cot_hbm,
    out, grad_in, grad_w, grad_b,
    weight, bias, cot, values, target, source_of, count, table_v, table, wide, adj, fwd, bwd,
    xg, adj_t, part, part_in, g_all, term, term_in,
    w_own, w_out, w_in, w_z, w_y, w_k, bias_k, bias_z, bias_y,
    in_sem, a_send, a_recv, b_send, b_recv, c_send, c_recv, d_send, d_recv, r_send, r_recv, ready,
):
    r = lax.axis_index("row")
    c = lax.axis_index("col")
    z = r // (2 * NY)
    xh = (r // NY) % 2
    y = r % NY
    k = xh * COLS + c
    inner = r % (2 * NY)

    def at_row(distance):
        return (lax.rem(r + distance + ROWS, ROWS), c)

    def at_col(step):
        return (r, lax.rem(c + step, COLS))

    def at_k(other):
        return (z * (2 * NY) + (other // COLS) * NY + y, lax.rem(other, COLS))

    def at_z(other):
        return (other * (2 * NY) + inner, c)

    def at_y(other):
        return (r - y + other, c)

    def ahead(me, step):
        return lax.rem(me + step, 8)

    def send(src, dst, send_sem, recv_sem, device):
        copy = pltpu.make_async_remote_copy(
            src_ref=src, dst_ref=dst, send_sem=send_sem, recv_sem=recv_sem,
            device_id=device, device_id_type=MESH,
        )
        copy.start()

    def landed(dst, sem):
        pltpu.make_async_copy(dst, dst, sem).wait()

    def total_of(parts):
        total = parts[0].astype(F32)
        for i in range(1, 8):
            total += parts[i].astype(F32)
        return total

    def local(i, src, dst):
        copy = pltpu.make_async_copy(src, dst, in_sem.at[i])
        copy.start()
        return copy

    barrier = pltpu.get_barrier_semaphore()
    for step in range(1, 8):
        for device in (at_k(ahead(k, step)), at_z(ahead(z, step)), at_y(ahead(y, step))):
            pl.semaphore_signal(barrier, inc=1, device_id=device, device_id_type=MESH)
    for distance in (-1, -2):
        pl.semaphore_signal(barrier, inc=1, device_id=at_row(distance), device_id_type=MESH)
    scalars = [
        local(0, target_hbm, target),
        local(1, source_hbm, source_of),
        local(2, count_hbm, count),
    ]
    own_x = local(3, x_hbm, xg.at[c])
    values_in = local(4, values_hbm, values)
    late = [local(5, weight_hbm, weight), local(6, bias_hbm, bias), local(7, cot_hbm, cot)]
    pl.semaphore_wait(barrier, 2 + 3 * 7)
    for distance in (1, 2):
        pl.semaphore_signal(ready, inc=1, device_id=at_row(distance), device_id_type=MESH)
    sibling = c + 1 - 2 * lax.rem(c, 2)
    facing = lax.rem(c + 2, COLS)
    behind = lax.rem(sibling + 2, COLS)
    pieces = [pl.ds(64 * i, 64) for i in range(4)]
    for i, rows in enumerate(pieces):
        send(x_hbm.at[rows], xg.at[c, rows], a_send, a_recv.at[i], (r, facing)
        )
    send(x_hbm, xg.at[c], a_send, a_recv.at[4], (r, sibling))
    for copy in scalars:
        copy.wait()
    lane = lax.broadcasted_iota(jnp.int32, (SLOTS, 128), 1)
    sub = lax.broadcasted_iota(jnp.int32, (SLOTS, 128), 0)
    in_row = jnp.full((SLOTS, 128), CELLS, jnp.int32)
    in_col = jnp.full((SLOTS, 128), CELLS, jnp.int32)
    for slot in range(SLOTS):
        cell = jnp.where(
            slot < count[0, 0], target[0, 0, slot] * (COLS * VB) + source_of[0, 0, slot], CELLS
        )
        in_row = jnp.where(lane == slot, cell, in_row)
        in_col = jnp.where(sub == slot, cell, in_col)
    table_v[0:1, :] = jnp.min(jnp.where(in_col == lane, sub, SLOTS), axis=0, keepdims=True)
    table_v[1:2, :] = jnp.min(
        jnp.where((in_col == in_row) & (sub > lane), sub, SLOTS), axis=0, keepdims=True
    )
    tabled = local(8, table_v, table)
    tabled.wait()
    values_in.wait()
    wide[SLOTS] = jnp.zeros((BLK, BLK), F32)
    for slot in range(SLOTS - 1, -1, -1):
        wide[slot] = values[0, 0, slot].astype(F32) + wide[table[1, slot]]
    for d in range(SPAN * VB):
        for e in range(COLS * VB):
            block = wide[table[0, d * (COLS * VB) + e]].astype(BF16)
            adj[d * BLK:(d + 1) * BLK, e * BLK:(e + 1) * BLK] = block
            adj_t[e * BLK:(e + 1) * BLK, d * BLK:(d + 1) * BLK] = block.T
    own_x.wait()
    landed(xg.at[sibling], a_recv.at[4])
    chip = c // 2
    near = xg[pl.ds(2 * chip, 2)].reshape(512, 256)
    near_lanes = pl.ds(pl.multiple_of(chip * 512, 512), 512)
    for offset in range(SPAN):
        fwd[offset] = dot(adj[offset * 256:(offset + 1) * 256, near_lanes], near)
    for i, rows in enumerate(pieces):
        landed(xg.at[facing, rows], a_recv.at[i])
        send(xg.at[facing, rows], xg.at[facing, rows], a_send, a_recv.at[5], (r, sibling))

    def row_block(i):
        return pl.ds(pl.multiple_of(i * 256, 256), 256)

    for offset in range(SPAN):
        fwd[offset] += dot(adj[offset * 256:(offset + 1) * 256, row_block(facing)], xg[facing])
    for copy in late:
        copy.wait()
    landed(xg.at[behind], a_recv.at[5])
    first, second = jnp.where(y < NY // 2, 0, 4), jnp.where(y < NY // 2, 1, 3)

    def mixed_at(offset):
        return fwd[offset] + dot(adj[row_block(offset), row_block(behind)], xg[behind])

    pl.semaphore_wait(ready, 2)
    for offset in (first, second, 4 - first, 4 - second):
        part[offset] = mixed_at(offset).astype(BF16)
        send(part.at[offset], part_in.at[offset], b_send, b_recv, at_row(offset - HALF))
    mixed = mixed_at(HALF)
    landed(part_in.at[pl.ds(0, 4)], b_recv)
    for offset in (1, 3, 0, 4):
        mixed += part_in[offset].astype(F32)

    high, low = split(mixed)
    pre = dot(high, weight[...]) + dot(low, weight[...]) + bias[...]
    sig = 1.0 / (1.0 + jnp.exp(-pre))
    exact = cot[...].astype(F32) * (sig * (1.0 + pre * (1.0 - sig)))
    grad = exact.astype(BF16)
    g_all[HALF] = grad
    def send_grad(src, dst, distance, arrived):
        send(g_all.at[src], g_all.at[dst], c_send, c_recv.at[arrived], at_row(distance)
        )


    across = (((0,), (0,)), ((), ()))
    w_term = lax.dot_general(high, grad, across, preferred_element_type=F32) + lax.dot_general(
        low, grad, across, preferred_element_type=F32
    )
    w_own[...] = w_term.reshape(8, 32, 256)
    w_out[...] = w_term.reshape(8, 32, 256).astype(BF16)
    bias_k[k] = jnp.sum(exact, axis=0, keepdims=True)
    for step in range(1, 8):
        other = ahead(k, step)
        send(w_out.at[other], w_in.at[k], r_send.at[0], r_recv.at[0], at_k(other)
        )
        send(bias_k.at[k], bias_k.at[k], r_send.at[1], r_recv.at[1], at_k(other)
        )
    send_grad(HALF, 1, 1, 0)
    send_grad(HALF, 3, -1, 1)
    w_in[k] = jnp.zeros((32, 256), BF16)
    out[...] = (pre * sig).astype(BF16)
    landed(w_in.at[pl.ds(0, 7)], r_recv.at[0])
    landed(bias_k.at[pl.ds(0, 7)], r_recv.at[1])
    w_y[y] = (w_own[k] + total_of(w_in)).astype(BF16)
    bias_y[y] = total_of(bias_k)
    for step in range(1, 8):
        other = ahead(y, step)
        send(w_y.at[y], w_y.at[y], r_send.at[2], r_recv.at[2], at_y(other)
        )
        send(bias_y.at[y], bias_y.at[y], r_send.at[3], r_recv.at[3], at_y(other)
        )
    landed(g_all.at[1], c_recv.at[0])
    send_grad(1, 0, 1, 2)
    landed(g_all.at[3], c_recv.at[1])
    send_grad(3, 4, -1, 2)
    close = g_all[pl.ds(1, 3)].reshape(768, 256)
    for j in range(COLS):
        bwd[j] = dot(adj_t[j * 256:(j + 1) * 256, 256:1024], close)
    landed(w_y.at[pl.ds(0, 7)], r_recv.at[2])
    landed(bias_y.at[pl.ds(0, 7)], r_recv.at[3])
    w_z[z] = total_of(w_y).astype(BF16)
    bias_z[z] = total_of(bias_y)
    for step in range(1, 8):
        other = ahead(z, step)
        send(w_z.at[z], w_z.at[z], r_send.at[4], r_recv.at[4], at_z(other)
        )
        send(bias_z.at[z], bias_z.at[z], r_send.at[5], r_recv.at[5], at_z(other)
        )
    landed(g_all.at[pl.ds(0, 2)], c_recv.at[2])

    def finished(j):
        rows = row_block(j)
        return bwd[j] + dot(adj_t[rows, 0:256], g_all[0]) + dot(adj_t[rows, 1024:1280], g_all[4])

    for i, other in enumerate((behind, sibling)):
        term[i] = finished(other).astype(BF16)
        send(term.at[i], term_in.at[i], d_send, d_recv.at[i], (r, sibling))
    bwd[facing] = finished(facing)
    bwd[c] = finished(c)
    landed(term_in.at[0], d_recv.at[0])
    term[2] = (bwd[facing] + term_in[0].astype(F32)).astype(BF16)
    send(term.at[2], term_in.at[2], d_send, d_recv.at[2], (r, facing))
    landed(w_z.at[pl.ds(0, 7)], r_recv.at[4])
    landed(bias_z.at[pl.ds(0, 7)], r_recv.at[5])
    normalizer = 1.0 / math.sqrt(256 * ROWS * COLS)
    w_k[k] = (total_of(w_z) * normalizer).astype(BF16)
    for step in range(1, 8):
        other = ahead(k, step)
        send(w_k.at[k], w_k.at[k], r_send.at[6], r_recv.at[6], at_k(other)
        )
    grad_b[...] = total_of(bias_z) * normalizer
    landed(term_in.at[1], d_recv.at[1])
    landed(term_in.at[2], d_recv.at[2])
    source = bwd[c] + term_in[1].astype(F32) + term_in[2].astype(F32)
    grad_in[...] = lax.dot_general(
        source.astype(BF16), weight[...], (((1,), (1,)), ((), ())), preferred_element_type=F32
    ).astype(BF16)
    landed(w_k.at[pl.ds(0, 7)], r_recv.at[6])
    grad_w[...] = w_k[...].reshape(256, 256)
    landed(xg.at[pl.ds(0, 3)], a_send)
    landed(part.at[pl.ds(0, 4)], b_send)
    landed(g_all.at[pl.ds(0, 4)], c_send)
    landed(term.at[pl.ds(0, 3)], d_send)
    for i, sent in enumerate((w_out, bias_k, w_y, bias_y, w_z, bias_z, w_k)):
        landed(sent.at[pl.ds(0, 7)], r_send.at[i])


def hand_over(out, grad_in, grad_w, grad_b, out_hbm, grad_in_hbm, grad_w_hbm, grad_b_hbm, wide_w, sems):
    copies = [
        pltpu.make_async_copy(src, dst, sems.at[i])
        for i, (src, dst) in enumerate(
            ((out, out_hbm), (grad_in, grad_in_hbm), (grad_b, grad_b_hbm), (wide_w, grad_w_hbm))
        )
    ]
    for copy in copies[:3]:
        copy.start()
    wide_w[...] = grad_w[...].astype(F32)
    copies[3].start()
    for copy in copies:
        copy.wait()


def shards(
    features, weight, bias, block_values, block_target, block_source, block_count, cotangent
):
    vmem = pl.BlockSpec(memory_space=pltpu.VMEM)
    hbm = pl.BlockSpec(memory_space=pltpu.HBM)
    dma = pltpu.SemaphoreType.DMA
    shapes = [
        jax.ShapeDtypeStruct((256, 256), BF16),
        jax.ShapeDtypeStruct((256, 256), BF16),
        jax.ShapeDtypeStruct((256, 256), BF16),
        jax.ShapeDtypeStruct((1, 256), F32),
    ]
    results = pl.pallas_call(
        layer,
        out_shape=shapes,
        in_specs=[hbm] * 8,
        out_specs=(vmem,) * 4,
        scratch_shapes=[
            pltpu.VMEM((256, 256), BF16),
            pltpu.VMEM((1, 256), F32),
            pltpu.VMEM((256, 256), BF16),
            pltpu.VMEM((1, 1, SLOTS, BLK, BLK), BF16),
            pltpu.SMEM((1, 1, SLOTS), jnp.int32),
            pltpu.SMEM((1, 1, SLOTS), jnp.int32),
            pltpu.SMEM((1, 1), jnp.int32),
            pltpu.VMEM((2, 128), jnp.int32),
            pltpu.SMEM((2, 128), jnp.int32),
            pltpu.VMEM((SLOTS + 1, BLK, BLK), F32),
            pltpu.VMEM((SPAN * 256, COLS * 256), BF16),
            pltpu.VMEM((SPAN, 256, 256), F32),
            pltpu.VMEM((COLS, 256, 256), F32),
            pltpu.VMEM((COLS, 256, 256), BF16),
            pltpu.VMEM((COLS * 256, SPAN * 256), BF16),
            pltpu.VMEM((SPAN, 256, 256), BF16),
            pltpu.VMEM((SPAN, 256, 256), BF16),
            pltpu.VMEM((SPAN, 256, 256), BF16),
            pltpu.VMEM((COLS, 256, 256), BF16),
            pltpu.VMEM((COLS, 256, 256), BF16),
            pltpu.VMEM((8, 32, 256), F32),
            pltpu.VMEM((8, 32, 256), BF16),
            pltpu.VMEM((8, 32, 256), BF16),
            pltpu.VMEM((8, 32, 256), BF16),
            pltpu.VMEM((8, 32, 256), BF16),
            pltpu.VMEM((8, 32, 256), BF16),
            pltpu.VMEM((8, 1, 256), F32),
            pltpu.VMEM((8, 1, 256), F32),
            pltpu.VMEM((8, 1, 256), F32),
            dma((9,)),
            dma,
            dma((6,)),
            dma,
            dma,
            dma,
            dma((3,)),
            dma,
            dma((3,)),
            dma((7,)),
            dma((7,)),
            pltpu.SemaphoreType.REGULAR,
        ],
        compiler_params=pltpu.CompilerParams(
            collective_id=0, has_side_effects=True, vmem_limit_bytes=VMEM_BYTES
        ),
        name="layer",
    )(
        features, weight, bias.reshape(1, 256), block_values, block_target, block_source, block_count, cotangent
    )
    output, grad_inputs, grad_weight, grad_bias = pl.pallas_call(
        hand_over,
        out_shape=[*shapes[:2], jax.ShapeDtypeStruct((256, 256), F32), shapes[3]],
        in_specs=[vmem] * 4,
        out_specs=(hbm,) * 4,
        scratch_shapes=[pltpu.VMEM((256, 256), F32), dma((4,))],
        compiler_params=pltpu.CompilerParams(vmem_limit_bytes=1 << 20),
        name="hand_over",
    )(*results)
    return output, grad_inputs, grad_weight, grad_bias.reshape(256)


def solution(mesh):
    return jax.shard_map(
        shards,
        mesh=mesh,
        in_specs=(
            P(("row", "col"), None),
            P(),
            P(),
            P("row", "col", None, None, None),
            P("row", "col", None),
            P("row", "col", None),
            P("row", "col"),
            P(("row", "col"), None),
        ),
        out_specs=(P(("row", "col"), None), P(("row", "col"), None), P(), P()),
        check_vma=False,
    )
```

```python
import math

import jax
import jax.numpy as jnp
from jax import lax
from jax.experimental import pallas as pl
from jax.experimental.pallas import tpu as pltpu
from jax.sharding import PartitionSpec as P

BLK = 128
HALF = 2
VB = 2
SPAN = 2 * HALF + 1
COLS = 4
ROWS = 128
NY = 8
NZ = 8
SLOTS = 32
VMEM_BYTES = 54810 << 10
CELLS = SPAN * VB * COLS * VB
MESH = pl.DeviceIdType.MESH
F32 = jnp.float32
BF16 = jnp.bfloat16


def dot(a, b):
    return jnp.dot(a, b, preferred_element_type=F32)


def split(value):
    high = value.astype(BF16)
    return high, (value - high.astype(F32)).astype(BF16)


def layer(
    x_hbm, weight_hbm, bias_hbm, values_hbm, target_hbm, source_hbm, count_hbm, cot_hbm,
    out, grad_in, grad_w, grad_b,
    weight, bias, cot, values, target, source_of, count, table_v, table, wide, adj, fwd, bwd,
    xg, adj_t, part, part_in, g_all, term, term_in,
    w_own, w_out, w_in, w_z, w_y, w_k, bias_k, bias_z, bias_y,
    in_sem, a_send, a_recv, b_send, b_recv, c_send, c_recv, d_send, d_recv, r_send, r_recv, ready,
):
    r = lax.axis_index("row")
    c = lax.axis_index("col")
    z = r // (2 * NY)
    xh = (r // NY) % 2
    y = r % NY
    k = xh * COLS + c
    inner = r % (2 * NY)

    def at_row(distance):
        return (lax.rem(r + distance + ROWS, ROWS), c)

    def at_col(step):
        return (r, lax.rem(c + step, COLS))

    def at_k(other):
        return (z * (2 * NY) + (other // COLS) * NY + y, lax.rem(other, COLS))

    def at_z(other):
        return (other * (2 * NY) + inner, c)

    def at_y(other):
        return (r - y + other, c)

    def ahead(me, step):
        return lax.rem(me + step, 8)

    def send(src, dst, send_sem, recv_sem, device):
        copy = pltpu.make_async_remote_copy(
            src_ref=src, dst_ref=dst, send_sem=send_sem, recv_sem=recv_sem,
            device_id=device, device_id_type=MESH,
        )
        copy.start()

    def landed(dst, sem):
        pltpu.make_async_copy(dst, dst, sem).wait()

    def total_of(parts):
        total = parts[0].astype(F32)
        for i in range(1, 8):
            total += parts[i].astype(F32)
        return total

    def local(i, src, dst):
        copy = pltpu.make_async_copy(src, dst, in_sem.at[i])
        copy.start()
        return copy

    def turn(place):
        return jnp.where(place < NY // 2, place, 3 * NY // 2 - 1 - place)

    def rank(row):
        return (4 * (row // (2 * NY)) + turn(lax.rem(row, NY))) * ROWS + row

    def signal(sem, device):
        pl.semaphore_signal(sem, inc=1, device_id=device, device_id_type=MESH)

    barrier = pltpu.get_barrier_semaphore()
    my_turn = turn(y)
    for step in range(1, COLS):
        signal(barrier, at_col(step))
    leads = []
    for distance in (1, -1, 2, -2):
        lead = rank(r) < rank(lax.rem(r + distance + ROWS, ROWS))
        leads.append(lead)
        pl.when(lead)(lambda distance=distance: signal(barrier, at_row(distance)))

    @pl.when(xh == 0)
    def _():
        for j in range(COLS):
            signal(barrier, at_k(COLS + j))

    @pl.loop(my_turn + 1, NY)
    def _(other):
        signal(barrier, at_y(turn(other)))

    @pl.loop(z + 1, NZ)
    def _(other):
        signal(barrier, at_z(other))

    followed = sum(jnp.where(lead, 0, 1) for lead in leads)
    scalars = [
        local(0, target_hbm, target),
        local(1, source_hbm, source_of),
        local(2, count_hbm, count),
    ]
    own_x = local(3, x_hbm, xg.at[c])
    values_in = local(4, values_hbm, values)
    late = [local(5, weight_hbm, weight), local(6, bias_hbm, bias), local(7, cot_hbm, cot)]
    pl.semaphore_wait(barrier, COLS - 1 + COLS * xh + my_turn + z + followed)
    sibling = c + 1 - 2 * lax.rem(c, 2)
    facing = lax.rem(c + 2, COLS)
    behind = lax.rem(sibling + 2, COLS)
    pieces = [pl.ds(64 * i, 64) for i in range(4)]
    for i, rows in enumerate(pieces):
        send(x_hbm.at[rows], xg.at[c, rows], a_send, a_recv.at[i], (r, facing)
        )
    send(x_hbm, xg.at[c], a_send, a_recv.at[4], (r, sibling))
    for distance, lead in zip((1, -1, 2, -2), leads):
        pl.when(jnp.logical_not(lead))(lambda distance=distance: signal(ready.at[0], at_row(distance)))

    @pl.when(xh == 1)
    def _():
        for j in range(COLS):
            signal(ready.at[1], at_k(j))

    @pl.loop(0, my_turn)
    def _(other):
        signal(ready.at[1], at_y(turn(other)))

    @pl.loop(0, z)
    def _(other):
        signal(ready.at[1], at_z(other))

    for copy in scalars:
        copy.wait()
    lane = lax.broadcasted_iota(jnp.int32, (SLOTS, 128), 1)
    sub = lax.broadcasted_iota(jnp.int32, (SLOTS, 128), 0)
    in_row = jnp.full((SLOTS, 128), CELLS, jnp.int32)
    in_col = jnp.full((SLOTS, 128), CELLS, jnp.int32)
    for slot in range(SLOTS):
        cell = jnp.where(
            slot < count[0, 0], target[0, 0, slot] * (COLS * VB) + source_of[0, 0, slot], CELLS
        )
        in_row = jnp.where(lane == slot, cell, in_row)
        in_col = jnp.where(sub == slot, cell, in_col)
    table_v[0:1, :] = jnp.min(jnp.where(in_col == lane, sub, SLOTS), axis=0, keepdims=True)
    table_v[1:2, :] = jnp.min(
        jnp.where((in_col == in_row) & (sub > lane), sub, SLOTS), axis=0, keepdims=True
    )
    tabled = local(8, table_v, table)
    tabled.wait()
    values_in.wait()
    wide[SLOTS] = jnp.zeros((BLK, BLK), F32)
    for slot in range(SLOTS - 1, -1, -1):
        wide[slot] = values[0, 0, slot].astype(F32) + wide[table[1, slot]]
    for d in range(SPAN * VB):
        for e in range(COLS * VB):
            block = wide[table[0, d * (COLS * VB) + e]].astype(BF16)
            adj[d * BLK:(d + 1) * BLK, e * BLK:(e + 1) * BLK] = block
            adj_t[e * BLK:(e + 1) * BLK, d * BLK:(d + 1) * BLK] = block.T
    own_x.wait()
    landed(xg.at[sibling], a_recv.at[4])
    chip = c // 2
    near = xg[pl.ds(2 * chip, 2)].reshape(512, 256)
    near_lanes = pl.ds(pl.multiple_of(chip * 512, 512), 512)
    for offset in range(SPAN):
        fwd[offset] = dot(adj[offset * 256:(offset + 1) * 256, near_lanes], near)
    for i, rows in enumerate(pieces):
        landed(xg.at[facing, rows], a_recv.at[i])
        send(xg.at[facing, rows], xg.at[facing, rows], a_send, a_recv.at[5], (r, sibling))

    def row_block(i):
        return pl.ds(pl.multiple_of(i * 256, 256), 256)

    for offset in range(SPAN):
        fwd[offset] += dot(adj[offset * 256:(offset + 1) * 256, row_block(facing)], xg[facing])
    for copy in late:
        copy.wait()
    landed(xg.at[behind], a_recv.at[5])
    first, second = jnp.where(y < NY // 2, 0, 4), jnp.where(y < NY // 2, 1, 3)

    def mixed_at(offset):
        return fwd[offset] + dot(adj[row_block(offset), row_block(behind)], xg[behind])

    pl.when(followed < 4)(lambda: pl.semaphore_wait(ready.at[0], 4 - followed))
    for offset in (first, second, 4 - first, 4 - second):
        part[offset] = mixed_at(offset).astype(BF16)
        send(part.at[offset], part_in.at[offset], b_send, b_recv, at_row(offset - HALF))
    mixed = mixed_at(HALF)
    landed(part_in.at[pl.ds(0, 4)], b_recv)
    for offset in (1, 3, 0, 4):
        mixed += part_in[offset].astype(F32)

    high, low = split(mixed)
    pre = dot(high, weight[...]) + dot(low, weight[...]) + bias[...]
    sig = 1.0 / (1.0 + jnp.exp(-pre))
    exact = cot[...].astype(F32) * (sig * (1.0 + pre * (1.0 - sig)))
    grad = exact.astype(BF16)
    g_all[HALF] = grad
    def send_grad(src, dst, distance, arrived):
        send(g_all.at[src], g_all.at[dst], c_send, c_recv.at[arrived], at_row(distance)
        )


    answers = COLS * (1 - xh) + (NY - 1 - my_turn) + (NZ - 1 - z)
    pl.when(answers > 0)(lambda: pl.semaphore_wait(ready.at[1], answers))
    across = (((0,), (0,)), ((), ()))
    w_term = lax.dot_general(high, grad, across, preferred_element_type=F32) + lax.dot_general(
        low, grad, across, preferred_element_type=F32
    )
    w_own[...] = w_term.reshape(8, 32, 256)
    w_out[...] = w_term.reshape(8, 32, 256).astype(BF16)
    bias_k[k] = jnp.sum(exact, axis=0, keepdims=True)
    for step in range(1, 8):
        other = ahead(k, step)
        send(w_out.at[other], w_in.at[k], r_send.at[0], r_recv.at[0], at_k(other)
        )
        send(bias_k.at[k], bias_k.at[k], r_send.at[1], r_recv.at[1], at_k(other)
        )
    send_grad(HALF, 1, 1, 0)
    send_grad(HALF, 3, -1, 1)
    w_in[k] = jnp.zeros((32, 256), BF16)
    out[...] = (pre * sig).astype(BF16)
    landed(w_in.at[pl.ds(0, 7)], r_recv.at[0])
    landed(bias_k.at[pl.ds(0, 7)], r_recv.at[1])
    w_y[y] = (w_own[k] + total_of(w_in)).astype(BF16)
    bias_y[y] = total_of(bias_k)
    for step in range(1, 8):
        other = ahead(y, step)
        send(w_y.at[y], w_y.at[y], r_send.at[2], r_recv.at[2], at_y(other)
        )
        send(bias_y.at[y], bias_y.at[y], r_send.at[3], r_recv.at[3], at_y(other)
        )
    landed(g_all.at[1], c_recv.at[0])
    send_grad(1, 0, 1, 2)
    landed(g_all.at[3], c_recv.at[1])
    send_grad(3, 4, -1, 2)
    close = g_all[pl.ds(1, 3)].reshape(768, 256)
    for j in range(COLS):
        bwd[j] = dot(adj_t[j * 256:(j + 1) * 256, 256:1024], close)
    landed(w_y.at[pl.ds(0, 7)], r_recv.at[2])
    landed(bias_y.at[pl.ds(0, 7)], r_recv.at[3])
    w_z[z] = total_of(w_y).astype(BF16)
    bias_z[z] = total_of(bias_y)
    for step in range(1, 8):
        other = ahead(z, step)
        send(w_z.at[z], w_z.at[z], r_send.at[4], r_recv.at[4], at_z(other)
        )
        send(bias_z.at[z], bias_z.at[z], r_send.at[5], r_recv.at[5], at_z(other)
        )
    landed(g_all.at[pl.ds(0, 2)], c_recv.at[2])

    def finished(j):
        rows = row_block(j)
        return bwd[j] + dot(adj_t[rows, 0:256], g_all[0]) + dot(adj_t[rows, 1024:1280], g_all[4])

    for i, other in enumerate((behind, sibling)):
        term[i] = finished(other).astype(BF16)
        send(term.at[i], term_in.at[i], d_send, d_recv.at[i], (r, sibling))
    bwd[facing] = finished(facing)
    bwd[c] = finished(c)
    landed(term_in.at[0], d_recv.at[0])
    term[2] = (bwd[facing] + term_in[0].astype(F32)).astype(BF16)
    send(term.at[2], term_in.at[2], d_send, d_recv.at[2], (r, facing))
    landed(w_z.at[pl.ds(0, 7)], r_recv.at[4])
    landed(bias_z.at[pl.ds(0, 7)], r_recv.at[5])
    normalizer = 1.0 / math.sqrt(256 * ROWS * COLS)
    w_k[k] = (total_of(w_z) * normalizer).astype(BF16)
    for step in range(1, 8):
        other = ahead(k, step)
        send(w_k.at[k], w_k.at[k], r_send.at[6], r_recv.at[6], at_k(other)
        )
    grad_b[...] = total_of(bias_z) * normalizer
    landed(term_in.at[1], d_recv.at[1])
    landed(term_in.at[2], d_recv.at[2])
    source = bwd[c] + term_in[1].astype(F32) + term_in[2].astype(F32)
    grad_in[...] = lax.dot_general(
        source.astype(BF16), weight[...], (((1,), (1,)), ((), ())), preferred_element_type=F32
    ).astype(BF16)
    landed(w_k.at[pl.ds(0, 7)], r_recv.at[6])
    grad_w[...] = w_k[...].reshape(256, 256)
    landed(xg.at[pl.ds(0, 3)], a_send)
    landed(part.at[pl.ds(0, 4)], b_send)
    landed(g_all.at[pl.ds(0, 4)], c_send)
    landed(term.at[pl.ds(0, 3)], d_send)
    for i, sent in enumerate((w_out, bias_k, w_y, bias_y, w_z, bias_z, w_k)):
        landed(sent.at[pl.ds(0, 7)], r_send.at[i])


def hand_over(out, grad_in, grad_w, grad_b, out_hbm, grad_in_hbm, grad_w_hbm, grad_b_hbm, wide_w, sems):
    copies = [
        pltpu.make_async_copy(src, dst, sems.at[i])
        for i, (src, dst) in enumerate(
            ((out, out_hbm), (grad_in, grad_in_hbm), (grad_b, grad_b_hbm), (wide_w, grad_w_hbm))
        )
    ]
    for copy in copies[:3]:
        copy.start()
    wide_w[...] = grad_w[...].astype(F32)
    copies[3].start()
    for copy in copies:
        copy.wait()


def shards(
    features, weight, bias, block_values, block_target, block_source, block_count, cotangent
):
    vmem = pl.BlockSpec(memory_space=pltpu.VMEM)
    hbm = pl.BlockSpec(memory_space=pltpu.HBM)
    dma = pltpu.SemaphoreType.DMA
    shapes = [
        jax.ShapeDtypeStruct((256, 256), BF16),
        jax.ShapeDtypeStruct((256, 256), BF16),
        jax.ShapeDtypeStruct((256, 256), BF16),
        jax.ShapeDtypeStruct((1, 256), F32),
    ]
    results = pl.pallas_call(
        layer,
        out_shape=shapes,
        in_specs=[hbm] * 8,
        out_specs=(vmem,) * 4,
        scratch_shapes=[
            pltpu.VMEM((256, 256), BF16),
            pltpu.VMEM((1, 256), F32),
            pltpu.VMEM((256, 256), BF16),
            pltpu.VMEM((1, 1, SLOTS, BLK, BLK), BF16),
            pltpu.SMEM((1, 1, SLOTS), jnp.int32),
            pltpu.SMEM((1, 1, SLOTS), jnp.int32),
            pltpu.SMEM((1, 1), jnp.int32),
            pltpu.VMEM((2, 128), jnp.int32),
            pltpu.SMEM((2, 128), jnp.int32),
            pltpu.VMEM((SLOTS + 1, BLK, BLK), F32),
            pltpu.VMEM((SPAN * 256, COLS * 256), BF16),
            pltpu.VMEM((SPAN, 256, 256), F32),
            pltpu.VMEM((COLS, 256, 256), F32),
            pltpu.VMEM((COLS, 256, 256), BF16),
            pltpu.VMEM((COLS * 256, SPAN * 256), BF16),
            pltpu.VMEM((SPAN, 256, 256), BF16),
            pltpu.VMEM((SPAN, 256, 256), BF16),
            pltpu.VMEM((SPAN, 256, 256), BF16),
            pltpu.VMEM((COLS, 256, 256), BF16),
            pltpu.VMEM((COLS, 256, 256), BF16),
            pltpu.VMEM((8, 32, 256), F32),
            pltpu.VMEM((8, 32, 256), BF16),
            pltpu.VMEM((8, 32, 256), BF16),
            pltpu.VMEM((8, 32, 256), BF16),
            pltpu.VMEM((8, 32, 256), BF16),
            pltpu.VMEM((8, 32, 256), BF16),
            pltpu.VMEM((8, 1, 256), F32),
            pltpu.VMEM((8, 1, 256), F32),
            pltpu.VMEM((8, 1, 256), F32),
            dma((9,)),
            dma,
            dma((6,)),
            dma,
            dma,
            dma,
            dma((3,)),
            dma,
            dma((3,)),
            dma((7,)),
            dma((7,)),
            pltpu.SemaphoreType.REGULAR((2,)),
        ],
        compiler_params=pltpu.CompilerParams(
            collective_id=0, has_side_effects=True, vmem_limit_bytes=VMEM_BYTES
        ),
        name="layer",
    )(
        features, weight, bias.reshape(1, 256), block_values, block_target, block_source, block_count, cotangent
    )
    output, grad_inputs, grad_weight, grad_bias = pl.pallas_call(
        hand_over,
        out_shape=[*shapes[:2], jax.ShapeDtypeStruct((256, 256), F32), shapes[3]],
        in_specs=[vmem] * 4,
        out_specs=(hbm,) * 4,
        scratch_shapes=[pltpu.VMEM((256, 256), F32), dma((4,))],
        compiler_params=pltpu.CompilerParams(vmem_limit_bytes=1 << 20),
        name="hand_over",
    )(*results)
    return output, grad_inputs, grad_weight, grad_bias.reshape(256)


def solution(mesh):
    return jax.shard_map(
        shards,
        mesh=mesh,
        in_specs=(
            P(("row", "col"), None),
            P(),
            P(),
            P("row", "col", None, None, None),
            P("row", "col", None),
            P("row", "col", None),
            P("row", "col"),
            P(("row", "col"), None),
        ),
        out_specs=(P(("row", "col"), None), P(("row", "col"), None), P(), P()),
        check_vma=False,
    )
```

```python
import math

import jax
import jax.numpy as jnp
from jax import lax
from jax.experimental import pallas as pl
from jax.experimental.pallas import tpu as pltpu
from jax.sharding import PartitionSpec as P

BLK = 128
HALF = 2
VB = 2
SPAN = 2 * HALF + 1
COLS = 4
ROWS = 128
NY = 8
NZ = 8
SLOTS = 32
VMEM_BYTES = 54810 << 10
CELLS = SPAN * VB * COLS * VB
MESH = pl.DeviceIdType.MESH
F32 = jnp.float32
BF16 = jnp.bfloat16


def dot(a, b):
    return jnp.dot(a, b, preferred_element_type=F32)


def split(value):
    high = value.astype(BF16)
    return high, (value - high.astype(F32)).astype(BF16)


def layer(
    x_hbm, weight_hbm, bias_hbm, values_hbm, target_hbm, source_hbm, count_hbm, cot_hbm,
    out, grad_in, grad_w, grad_b,
    weight, bias, cot, values, target, source_of, count, table_v, table, wide, adj, fwd, bwd,
    xg, adj_t, part, part_in, g_all, term, term_in,
    w_own, w_out, w_in, w_z, w_y, w_k, bias_k, bias_z, bias_y,
    in_sem, a_send, a_recv, b_send, b_recv, c_send, c_recv, d_send, d_recv, r_send, r_recv, ready,
):
    r = lax.axis_index("row")
    c = lax.axis_index("col")
    z = r // (2 * NY)
    xh = (r // NY) % 2
    y = r % NY
    k = xh * COLS + c
    inner = r % (2 * NY)

    def at_row(distance):
        return (lax.rem(r + distance + ROWS, ROWS), c)

    def at_col(step):
        return (r, lax.rem(c + step, COLS))

    def at_k(other):
        return (z * (2 * NY) + (other // COLS) * NY + y, lax.rem(other, COLS))

    def at_z(other):
        return (other * (2 * NY) + inner, c)

    def at_y(other):
        return (r - y + other, c)

    def ahead(me, step):
        return lax.rem(me + step, 8)

    def send(src, dst, send_sem, recv_sem, device):
        copy = pltpu.make_async_remote_copy(
            src_ref=src, dst_ref=dst, send_sem=send_sem, recv_sem=recv_sem,
            device_id=device, device_id_type=MESH,
        )
        copy.start()

    def landed(dst, sem):
        pltpu.make_async_copy(dst, dst, sem).wait()

    def total_of(parts):
        total = parts[0].astype(F32)
        for i in range(1, 8):
            total += parts[i].astype(F32)
        return total

    def local(i, src, dst):
        copy = pltpu.make_async_copy(src, dst, in_sem.at[i])
        copy.start()
        return copy

    def turn(place):
        return jnp.where(place < NY // 2, place, 3 * NY // 2 - 1 - place)

    def rank(row):
        return (4 * (row // (2 * NY)) + turn(lax.rem(row, NY))) * ROWS + row

    def signal(sem, device):
        pl.semaphore_signal(sem, inc=1, device_id=device, device_id_type=MESH)

    barrier = pltpu.get_barrier_semaphore()
    my_turn = turn(y)
    for step in range(1, COLS):
        signal(barrier, at_col(step))
    leads = []
    for distance in (1, -1):
        lead = rank(r) < rank(lax.rem(r + distance + ROWS, ROWS))
        leads.append(lead)
        pl.when(lead)(lambda distance=distance: signal(barrier, at_row(distance)))

    @pl.when(xh == 0)
    def _():
        for j in range(COLS):
            signal(barrier, at_k(COLS + j))

    @pl.loop(my_turn + 1, NY)
    def _(other):
        signal(barrier, at_y(turn(other)))

    @pl.loop(z + 1, NZ)
    def _(other):
        signal(barrier, at_z(other))

    followed = sum(jnp.where(lead, 0, 1) for lead in leads)
    scalars = [
        local(0, target_hbm, target),
        local(1, source_hbm, source_of),
        local(2, count_hbm, count),
    ]
    own_x = local(3, x_hbm, xg.at[c])
    values_in = local(4, values_hbm, values)
    late = [local(5, weight_hbm, weight), local(6, bias_hbm, bias), local(7, cot_hbm, cot)]
    pl.semaphore_wait(barrier, COLS - 1 + COLS * xh + my_turn + z + followed)
    sibling = c + 1 - 2 * lax.rem(c, 2)
    facing = lax.rem(c + 2, COLS)
    behind = lax.rem(sibling + 2, COLS)
    pieces = [pl.ds(64 * i, 64) for i in range(4)]
    for i, rows in enumerate(pieces):
        send(x_hbm.at[rows], xg.at[c, rows], a_send, a_recv.at[i], (r, facing))
    send(x_hbm.at[pieces[3]], xg.at[c, pieces[3]], a_send, a_recv.at[5], (r, behind))
    send(x_hbm, xg.at[c], a_send, a_recv.at[4], (r, sibling))
    for distance, lead in zip((1, -1), leads):
        pl.when(jnp.logical_not(lead))(lambda distance=distance: signal(ready.at[0], at_row(distance)))

    @pl.when(xh == 1)
    def _():
        for j in range(COLS):
            signal(ready.at[1], at_k(j))

    @pl.loop(0, my_turn)
    def _(other):
        signal(ready.at[1], at_y(turn(other)))

    @pl.loop(0, z)
    def _(other):
        signal(ready.at[1], at_z(other))

    for copy in scalars:
        copy.wait()
    lane = lax.broadcasted_iota(jnp.int32, (SLOTS, 128), 1)
    sub = lax.broadcasted_iota(jnp.int32, (SLOTS, 128), 0)
    in_row = jnp.full((SLOTS, 128), CELLS, jnp.int32)
    in_col = jnp.full((SLOTS, 128), CELLS, jnp.int32)
    for slot in range(SLOTS):
        cell = jnp.where(
            slot < count[0, 0], target[0, 0, slot] * (COLS * VB) + source_of[0, 0, slot], CELLS
        )
        in_row = jnp.where(lane == slot, cell, in_row)
        in_col = jnp.where(sub == slot, cell, in_col)
    table_v[0:1, :] = jnp.min(jnp.where(in_col == lane, sub, SLOTS), axis=0, keepdims=True)
    table_v[1:2, :] = jnp.min(
        jnp.where((in_col == in_row) & (sub > lane), sub, SLOTS), axis=0, keepdims=True
    )
    tabled = local(8, table_v, table)
    tabled.wait()
    values_in.wait()
    wide[SLOTS] = jnp.zeros((BLK, BLK), F32)
    for slot in range(SLOTS - 1, -1, -1):
        wide[slot] = values[0, 0, slot].astype(F32) + wide[table[1, slot]]
    for d in range(SPAN * VB):
        for e in range(COLS * VB):
            block = wide[table[0, d * (COLS * VB) + e]].astype(BF16)
            adj[d * BLK:(d + 1) * BLK, e * BLK:(e + 1) * BLK] = block
            adj_t[e * BLK:(e + 1) * BLK, d * BLK:(d + 1) * BLK] = block.T
    own_x.wait()
    landed(xg.at[sibling], a_recv.at[4])
    chip = c // 2
    near = xg[pl.ds(2 * chip, 2)].reshape(512, 256)
    near_lanes = pl.ds(pl.multiple_of(chip * 512, 512), 512)
    for offset in range(SPAN):
        fwd[offset] = dot(adj[offset * 256:(offset + 1) * 256, near_lanes], near)
    for i, rows in enumerate(pieces):
        landed(xg.at[facing, rows], a_recv.at[i])
        if i < 3:
            send(xg.at[facing, rows], xg.at[facing, rows], a_send, a_recv.at[5], (r, sibling))

    def row_block(i):
        return pl.ds(pl.multiple_of(i * 256, 256), 256)

    for offset in range(SPAN):
        fwd[offset] += dot(adj[offset * 256:(offset + 1) * 256, row_block(facing)], xg[facing])
    for copy in late:
        copy.wait()
    landed(xg.at[behind], a_recv.at[5])
    first = jnp.where(y < NY // 2, 0, 4)

    def mixed_at(offset):
        return fwd[offset] + dot(adj[row_block(offset), row_block(behind)], xg[behind])

    pl.when(followed < 2)(lambda: pl.semaphore_wait(ready.at[0], 2 - followed))
    for offset in (first, 4 - first):
        part[offset] = mixed_at(offset).astype(BF16)
        send(part.at[offset], part_in.at[offset], b_send, b_recv.at[offset // 4], at_row(offset // 2 - 1))
    for offset in (1, 3, HALF):
        fwd[offset] = mixed_at(offset)
    for offset in (first, 4 - first):
        landed(part_in.at[offset], b_recv.at[offset // 4])
        onward = offset // 2 + 1
        part[onward] = (fwd[onward] + part_in[offset].astype(F32)).astype(BF16)
        send(part.at[onward], part_in.at[onward], b_send, b_recv.at[2], at_row(offset // 2 - 1))
    landed(part_in.at[pl.ds(0, 2)], b_recv.at[2])
    mixed = fwd[HALF] + part_in[1].astype(F32) + part_in[3].astype(F32)
    high, low = split(mixed)
    pre = dot(high, weight[...]) + dot(low, weight[...]) + bias[...]
    sig = 1.0 / (1.0 + jnp.exp(-pre))
    exact = cot[...].astype(F32) * (sig * (1.0 + pre * (1.0 - sig)))
    grad = exact.astype(BF16)
    g_all[HALF] = grad
    def send_grad(src, dst, distance, arrived):
        send(g_all.at[src], g_all.at[dst], c_send, c_recv.at[arrived], at_row(distance))


    answers = COLS * (1 - xh) + (NY - 1 - my_turn) + (NZ - 1 - z)
    pl.when(answers > 0)(lambda: pl.semaphore_wait(ready.at[1], answers))
    across = (((0,), (0,)), ((), ()))
    w_term = lax.dot_general(high, grad, across, preferred_element_type=F32) + lax.dot_general(
        low, grad, across, preferred_element_type=F32
    )
    w_own[...] = w_term.reshape(8, 32, 256)
    w_out[...] = w_term.reshape(8, 32, 256).astype(BF16)
    bias_k[k] = jnp.sum(exact, axis=0, keepdims=True)
    for step in range(1, 8):
        other = ahead(k, step)
        send(w_out.at[other], w_in.at[k], r_send.at[0], r_recv.at[0], at_k(other))
        send(bias_k.at[k], bias_k.at[k], r_send.at[1], r_recv.at[1], at_k(other))
    send_grad(HALF, 1, 1, 0)
    send_grad(HALF, 3, -1, 1)
    w_in[k] = jnp.zeros((32, 256), BF16)
    out[...] = (pre * sig).astype(BF16)
    landed(w_in.at[pl.ds(0, 7)], r_recv.at[0])
    landed(bias_k.at[pl.ds(0, 7)], r_recv.at[1])
    w_y[y] = (w_own[k] + total_of(w_in)).astype(BF16)
    bias_y[y] = total_of(bias_k)
    for step in range(1, 8):
        other = ahead(y, step)
        send(w_y.at[y], w_y.at[y], r_send.at[2], r_recv.at[2], at_y(other))
        send(bias_y.at[y], bias_y.at[y], r_send.at[3], r_recv.at[3], at_y(other))
    landed(g_all.at[1], c_recv.at[0])
    send_grad(1, 0, 1, 2)
    landed(g_all.at[3], c_recv.at[1])
    send_grad(3, 4, -1, 2)
    close = g_all[pl.ds(1, 3)].reshape(768, 256)
    for j in range(COLS):
        bwd[j] = dot(adj_t[j * 256:(j + 1) * 256, 256:1024], close)
    landed(w_y.at[pl.ds(0, 7)], r_recv.at[2])
    landed(bias_y.at[pl.ds(0, 7)], r_recv.at[3])
    w_z[z] = total_of(w_y).astype(BF16)
    bias_z[z] = total_of(bias_y)
    for step in range(1, 8):
        other = ahead(z, step)
        send(w_z.at[z], w_z.at[z], r_send.at[4], r_recv.at[4], at_z(other))
        send(bias_z.at[z], bias_z.at[z], r_send.at[5], r_recv.at[5], at_z(other))
    landed(g_all.at[pl.ds(0, 2)], c_recv.at[2])

    def finished(j):
        rows = row_block(j)
        return bwd[j] + dot(adj_t[rows, 0:256], g_all[0]) + dot(adj_t[rows, 1024:1280], g_all[4])

    for i, other in enumerate((behind, sibling)):
        term[i] = finished(other).astype(BF16)
        send(term.at[i], term_in.at[i], d_send, d_recv.at[i], (r, sibling))
    bwd[facing] = finished(facing)
    bwd[c] = finished(c)
    landed(term_in.at[0], d_recv.at[0])
    term[2] = (bwd[facing] + term_in[0].astype(F32)).astype(BF16)
    send(term.at[2], term_in.at[2], d_send, d_recv.at[2], (r, facing))
    landed(w_z.at[pl.ds(0, 7)], r_recv.at[4])
    landed(bias_z.at[pl.ds(0, 7)], r_recv.at[5])
    normalizer = 1.0 / math.sqrt(256 * ROWS * COLS)
    w_k[k] = (total_of(w_z) * normalizer).astype(BF16)
    for step in range(1, 8):
        other = ahead(k, step)
        send(w_k.at[k], w_k.at[k], r_send.at[6], r_recv.at[6], at_k(other))
    grad_b[...] = total_of(bias_z) * normalizer
    landed(term_in.at[1], d_recv.at[1])
    landed(term_in.at[2], d_recv.at[2])
    source = bwd[c] + term_in[1].astype(F32) + term_in[2].astype(F32)
    grad_in[...] = lax.dot_general(
        source.astype(BF16), weight[...], (((1,), (1,)), ((), ())), preferred_element_type=F32
    ).astype(BF16)
    landed(w_k.at[pl.ds(0, 7)], r_recv.at[6])
    grad_w[...] = w_k[...].reshape(256, 256)
    landed(xg.at[pl.ds(0, 3)], a_send)
    landed(part.at[pl.ds(0, 4)], b_send)
    landed(g_all.at[pl.ds(0, 4)], c_send)
    landed(term.at[pl.ds(0, 3)], d_send)
    for i, sent in enumerate((w_out, bias_k, w_y, bias_y, w_z, bias_z, w_k)):
        landed(sent.at[pl.ds(0, 7)], r_send.at[i])


def hand_over(out, grad_in, grad_w, grad_b, out_hbm, grad_in_hbm, grad_w_hbm, grad_b_hbm, wide_w, sems):
    copies = [
        pltpu.make_async_copy(src, dst, sems.at[i])
        for i, (src, dst) in enumerate(
            ((out, out_hbm), (grad_in, grad_in_hbm), (grad_b, grad_b_hbm), (wide_w, grad_w_hbm)))
    ]
    for copy in copies[:3]:
        copy.start()
    wide_w[...] = grad_w[...].astype(F32)
    copies[3].start()
    for copy in copies:
        copy.wait()


def shards(
    features, weight, bias, block_values, block_target, block_source, block_count, cotangent
):
    vmem = pl.BlockSpec(memory_space=pltpu.VMEM)
    hbm = pl.BlockSpec(memory_space=pltpu.HBM)
    dma = pltpu.SemaphoreType.DMA
    shapes = [
        jax.ShapeDtypeStruct((256, 256), BF16),
        jax.ShapeDtypeStruct((256, 256), BF16),
        jax.ShapeDtypeStruct((256, 256), BF16),
        jax.ShapeDtypeStruct((1, 256), F32),
    ]
    results = pl.pallas_call(
        layer,
        out_shape=shapes,
        in_specs=[hbm] * 8,
        out_specs=(vmem,) * 4,
        scratch_shapes=[
            pltpu.VMEM((256, 256), BF16),
            pltpu.VMEM((1, 256), F32),
            pltpu.VMEM((256, 256), BF16),
            pltpu.VMEM((1, 1, SLOTS, BLK, BLK), BF16),
            pltpu.SMEM((1, 1, SLOTS), jnp.int32),
            pltpu.SMEM((1, 1, SLOTS), jnp.int32),
            pltpu.SMEM((1, 1), jnp.int32),
            pltpu.VMEM((2, 128), jnp.int32),
            pltpu.SMEM((2, 128), jnp.int32),
            pltpu.VMEM((SLOTS + 1, BLK, BLK), F32),
            pltpu.VMEM((SPAN * 256, COLS * 256), BF16),
            pltpu.VMEM((SPAN, 256, 256), F32),
            pltpu.VMEM((COLS, 256, 256), F32),
            pltpu.VMEM((COLS, 256, 256), BF16),
            pltpu.VMEM((COLS * 256, SPAN * 256), BF16),
            pltpu.VMEM((SPAN, 256, 256), BF16),
            pltpu.VMEM((SPAN, 256, 256), BF16),
            pltpu.VMEM((SPAN, 256, 256), BF16),
            pltpu.VMEM((COLS, 256, 256), BF16),
            pltpu.VMEM((COLS, 256, 256), BF16),
            pltpu.VMEM((8, 32, 256), F32),
            pltpu.VMEM((8, 32, 256), BF16),
            pltpu.VMEM((8, 32, 256), BF16),
            pltpu.VMEM((8, 32, 256), BF16),
            pltpu.VMEM((8, 32, 256), BF16),
            pltpu.VMEM((8, 32, 256), BF16),
            pltpu.VMEM((8, 1, 256), F32),
            pltpu.VMEM((8, 1, 256), F32),
            pltpu.VMEM((8, 1, 256), F32),
            dma((9,)),
            dma,
            dma((6,)),
            dma,
            dma((3,)),
            dma,
            dma((3,)),
            dma,
            dma((3,)),
            dma((7,)),
            dma((7,)),
            pltpu.SemaphoreType.REGULAR((2,)),
        ],
        compiler_params=pltpu.CompilerParams(
            collective_id=0, has_side_effects=True, vmem_limit_bytes=VMEM_BYTES
        ),
        name="layer",
    )(
        features, weight, bias.reshape(1, 256), block_values, block_target, block_source, block_count, cotangent
    )
    output, grad_inputs, grad_weight, grad_bias = pl.pallas_call(
        hand_over,
        out_shape=[*shapes[:2], jax.ShapeDtypeStruct((256, 256), F32), shapes[3]],
        in_specs=[vmem] * 4,
        out_specs=(hbm,) * 4,
        scratch_shapes=[pltpu.VMEM((256, 256), F32), dma((4,))],
        compiler_params=pltpu.CompilerParams(vmem_limit_bytes=1 << 20),
        name="hand_over",
    )(*results)
    return output, grad_inputs, grad_weight, grad_bias.reshape(256)


def solution(mesh):
    return jax.shard_map(
        shards,
        mesh=mesh,
        in_specs=(
            P(("row", "col"), None),
            P(),
            P(),
            P("row", "col", None, None, None),
            P("row", "col", None),
            P("row", "col", None),
            P("row", "col"),
            P(("row", "col"), None),
        ),
        out_specs=(P(("row", "col"), None), P(("row", "col"), None), P(), P()),
        check_vma=False,
    )
```

```python
import math

import jax
import jax.numpy as jnp
from jax import lax
from jax.experimental import pallas as pl
from jax.experimental.pallas import tpu as pltpu
from jax.sharding import PartitionSpec as P

BLK = 128
HALF = 2
VB = 2
SPAN = 2 * HALF + 1
COLS = 4
ROWS = 128
NY = 8
NZ = 8
SLOTS = 32
FAR_FIRST = (4, 3, 5, 2, 6, 1, 7)
VMEM_BYTES = 54810 << 10
CELLS = SPAN * VB * COLS * VB
MESH = pl.DeviceIdType.MESH
F32 = jnp.float32
BF16 = jnp.bfloat16


def dot(a, b):
    return jnp.dot(a, b, preferred_element_type=F32)


def split(value):
    high = value.astype(BF16)
    return high, (value - high.astype(F32)).astype(BF16)


def layer(
    x_hbm, weight_hbm, bias_hbm, values_hbm, target_hbm, source_hbm, count_hbm, cot_hbm,
    out, grad_in, grad_w, grad_b,
    weight, bias, cot, values, target, source_of, count, table_v, table, wide, adj, fwd, bwd,
    xg, adj_t, part, part_in, g_all, term, term_in,
    w_own, w_out, w_in, w_z, w_y, w_k, bias_k, bias_z, bias_y,
    in_sem, a_send, a_recv, b_send, b_recv, c_send, c_recv, d_send, d_recv, r_send, r_recv, ready,
):
    r = lax.axis_index("row")
    c = lax.axis_index("col")
    z = r // (2 * NY)
    xh = (r // NY) % 2
    y = r % NY
    k = xh * COLS + c
    inner = r % (2 * NY)

    def at_row(distance):
        return (lax.rem(r + distance + ROWS, ROWS), c)

    def at_col(step):
        return (r, lax.rem(c + step, COLS))

    def at_k(other):
        return (z * (2 * NY) + (other // COLS) * NY + y, lax.rem(other, COLS))

    def at_z(other):
        return (other * (2 * NY) + inner, c)

    def at_y(other):
        return (r - y + other, c)

    def ahead(me, step):
        return lax.rem(me + step, 8)

    def send(src, dst, send_sem, recv_sem, device):
        copy = pltpu.make_async_remote_copy(
            src_ref=src, dst_ref=dst, send_sem=send_sem, recv_sem=recv_sem,
            device_id=device, device_id_type=MESH,
        )
        copy.start()

    def landed(dst, sem):
        pltpu.make_async_copy(dst, dst, sem).wait()

    def total_of(parts):
        total = parts[0].astype(F32)
        for i in range(1, 8):
            total += parts[i].astype(F32)
        return total

    def local(i, src, dst):
        copy = pltpu.make_async_copy(src, dst, in_sem.at[i])
        copy.start()
        return copy

    def turn(place):
        return jnp.where(place < NY // 2, place, 3 * NY // 2 - 1 - place)

    def rank(row):
        return (4 * (row // (2 * NY)) + turn(lax.rem(row, NY))) * ROWS + row

    def signal(sem, device):
        pl.semaphore_signal(sem, inc=1, device_id=device, device_id_type=MESH)

    barrier = pltpu.get_barrier_semaphore()
    my_turn = turn(y)
    for step in range(1, COLS):
        signal(barrier, at_col(step))
    leads = []
    for distance in (1, -1):
        lead = rank(r) < rank(lax.rem(r + distance + ROWS, ROWS))
        leads.append(lead)
        pl.when(lead)(lambda distance=distance: signal(barrier, at_row(distance)))

    @pl.when(xh == 0)
    def _():
        for j in range(COLS):
            signal(barrier, at_k(COLS + j))

    @pl.loop(my_turn + 1, NY)
    def _(other):
        signal(barrier, at_y(turn(other)))

    @pl.loop(z + 1, NZ)
    def _(other):
        signal(barrier, at_z(other))

    followed = sum(jnp.where(lead, 0, 1) for lead in leads)
    scalars = [
        local(0, target_hbm, target),
        local(1, source_hbm, source_of),
        local(2, count_hbm, count),
    ]
    own_x = local(3, x_hbm, xg.at[c])
    values_in = local(4, values_hbm, values)
    late = [local(5, weight_hbm, weight), local(6, bias_hbm, bias), local(7, cot_hbm, cot)]
    pl.semaphore_wait(barrier, COLS - 1 + COLS * xh + my_turn + z + followed)
    sibling = c + 1 - 2 * lax.rem(c, 2)
    facing = lax.rem(c + 2, COLS)
    behind = lax.rem(sibling + 2, COLS)
    pieces = [pl.ds(64 * i, 64) for i in range(4)]
    for i, rows in enumerate(pieces):
        send(x_hbm.at[rows], xg.at[c, rows], a_send, a_recv.at[i], (r, facing))
    send(x_hbm.at[pieces[3]], xg.at[c, pieces[3]], a_send, a_recv.at[5], (r, behind))
    send(x_hbm, xg.at[c], a_send, a_recv.at[4], (r, sibling))
    for distance, lead in zip((1, -1), leads):
        pl.when(jnp.logical_not(lead))(lambda distance=distance: signal(ready.at[0], at_row(distance)))

    @pl.when(xh == 1)
    def _():
        for j in range(COLS):
            signal(ready.at[1], at_k(j))

    @pl.loop(0, my_turn)
    def _(other):
        signal(ready.at[1], at_y(turn(other)))

    @pl.loop(0, z)
    def _(other):
        signal(ready.at[1], at_z(other))

    for copy in scalars:
        copy.wait()
    lane = lax.broadcasted_iota(jnp.int32, (SLOTS, 128), 1)
    sub = lax.broadcasted_iota(jnp.int32, (SLOTS, 128), 0)
    in_row = jnp.full((SLOTS, 128), CELLS, jnp.int32)
    in_col = jnp.full((SLOTS, 128), CELLS, jnp.int32)
    for slot in range(SLOTS):
        cell = jnp.where(
            slot < count[0, 0], target[0, 0, slot] * (COLS * VB) + source_of[0, 0, slot], CELLS
        )
        in_row = jnp.where(lane == slot, cell, in_row)
        in_col = jnp.where(sub == slot, cell, in_col)
    table_v[0:1, :] = jnp.min(jnp.where(in_col == lane, sub, SLOTS), axis=0, keepdims=True)
    table_v[1:2, :] = jnp.min(
        jnp.where((in_col == in_row) & (sub > lane), sub, SLOTS), axis=0, keepdims=True
    )
    tabled = local(8, table_v, table)
    tabled.wait()
    values_in.wait()
    wide[SLOTS] = jnp.zeros((BLK, BLK), F32)
    for slot in range(SLOTS - 1, -1, -1):
        wide[slot] = values[0, 0, slot].astype(F32) + wide[table[1, slot]]
    for d in range(SPAN * VB):
        for e in range(COLS * VB):
            block = wide[table[0, d * (COLS * VB) + e]].astype(BF16)
            adj[d * BLK:(d + 1) * BLK, e * BLK:(e + 1) * BLK] = block
            adj_t[e * BLK:(e + 1) * BLK, d * BLK:(d + 1) * BLK] = block.T
    own_x.wait()
    landed(xg.at[sibling], a_recv.at[4])
    chip = c // 2
    near = xg[pl.ds(2 * chip, 2)].reshape(512, 256)
    near_lanes = pl.ds(pl.multiple_of(chip * 512, 512), 512)
    for offset in range(SPAN):
        fwd[offset] = dot(adj[offset * 256:(offset + 1) * 256, near_lanes], near)
    for i, rows in enumerate(pieces):
        landed(xg.at[facing, rows], a_recv.at[i])
        if i < 3:
            send(xg.at[facing, rows], xg.at[facing, rows], a_send, a_recv.at[5], (r, sibling))

    def row_block(i):
        return pl.ds(pl.multiple_of(i * 256, 256), 256)

    for offset in range(SPAN):
        fwd[offset] += dot(adj[offset * 256:(offset + 1) * 256, row_block(facing)], xg[facing])
    for copy in late:
        copy.wait()
    landed(xg.at[behind], a_recv.at[5])
    first = jnp.where(y < NY // 2, 0, 4)

    def mixed_at(offset):
        return fwd[offset] + dot(adj[row_block(offset), row_block(behind)], xg[behind])

    pl.when(followed < 2)(lambda: pl.semaphore_wait(ready.at[0], 2 - followed))
    for offset in (first, 4 - first):
        part[offset] = mixed_at(offset).astype(BF16)
        send(part.at[offset], part_in.at[offset], b_send, b_recv.at[offset // 4], at_row(offset // 2 - 1))
    for offset in (1, 3, HALF):
        fwd[offset] = mixed_at(offset)
    for offset in (first, 4 - first):
        landed(part_in.at[offset], b_recv.at[offset // 4])
        onward = offset // 2 + 1
        part[onward] = (fwd[onward] + part_in[offset].astype(F32)).astype(BF16)
        send(part.at[onward], part_in.at[onward], b_send, b_recv.at[2], at_row(offset // 2 - 1))
    landed(part_in.at[pl.ds(0, 2)], b_recv.at[2])
    mixed = fwd[HALF] + part_in[1].astype(F32) + part_in[3].astype(F32)
    high, low = split(mixed)
    pre = dot(high, weight[...]) + dot(low, weight[...]) + bias[...]
    sig = 1.0 / (1.0 + jnp.exp(-pre))
    exact = cot[...].astype(F32) * (sig * (1.0 + pre * (1.0 - sig)))
    grad = exact.astype(BF16)
    g_all[HALF] = grad
    def send_grad(src, dst, distance, arrived):
        send(g_all.at[src], g_all.at[dst], c_send, c_recv.at[arrived], at_row(distance))


    send_grad(HALF, 1, 1, 0)
    send_grad(HALF, 3, -1, 1)
    answers = COLS * (1 - xh) + (NY - 1 - my_turn) + (NZ - 1 - z)
    pl.when(answers > 0)(lambda: pl.semaphore_wait(ready.at[1], answers))
    across = (((0,), (0,)), ((), ()))
    w_term = lax.dot_general(high, grad, across, preferred_element_type=F32) + lax.dot_general(
        low, grad, across, preferred_element_type=F32
    )
    w_own[...] = w_term.reshape(8, 32, 256)
    w_out[...] = w_term.reshape(8, 32, 256).astype(BF16)
    bias_k[k] = jnp.sum(exact, axis=0, keepdims=True)
    for step in FAR_FIRST:
        other = ahead(k, step)
        send(w_out.at[other], w_in.at[k], r_send.at[0], r_recv.at[0], at_k(other))
        send(bias_k.at[k], bias_k.at[k], r_send.at[1], r_recv.at[1], at_k(other))
    w_in[k] = jnp.zeros((32, 256), BF16)
    out[...] = (pre * sig).astype(BF16)
    landed(w_in.at[pl.ds(0, 7)], r_recv.at[0])
    landed(bias_k.at[pl.ds(0, 7)], r_recv.at[1])
    w_y[y] = (w_own[k] + total_of(w_in)).astype(BF16)
    bias_y[y] = total_of(bias_k)
    for step in FAR_FIRST:
        other = ahead(y, step)
        send(w_y.at[y], w_y.at[y], r_send.at[2], r_recv.at[2], at_y(other))
        send(bias_y.at[y], bias_y.at[y], r_send.at[3], r_recv.at[3], at_y(other))
    landed(g_all.at[1], c_recv.at[0])
    send_grad(1, 0, 1, 2)
    landed(g_all.at[3], c_recv.at[1])
    send_grad(3, 4, -1, 2)
    close = g_all[pl.ds(1, 3)].reshape(768, 256)
    for j in range(COLS):
        bwd[j] = dot(adj_t[j * 256:(j + 1) * 256, 256:1024], close)
    landed(w_y.at[pl.ds(0, 7)], r_recv.at[2])
    landed(bias_y.at[pl.ds(0, 7)], r_recv.at[3])
    w_z[z] = total_of(w_y).astype(BF16)
    bias_z[z] = total_of(bias_y)
    for step in FAR_FIRST:
        other = ahead(z, step)
        send(w_z.at[z], w_z.at[z], r_send.at[4], r_recv.at[4], at_z(other))
        send(bias_z.at[z], bias_z.at[z], r_send.at[5], r_recv.at[5], at_z(other))
    landed(g_all.at[pl.ds(0, 2)], c_recv.at[2])

    def finished(j):
        rows = row_block(j)
        return bwd[j] + dot(adj_t[rows, 0:256], g_all[0]) + dot(adj_t[rows, 1024:1280], g_all[4])

    for i, other in enumerate((behind, sibling)):
        term[i] = finished(other).astype(BF16)
        send(term.at[i], term_in.at[i], d_send, d_recv.at[i], (r, sibling))
    bwd[facing] = finished(facing)
    bwd[c] = finished(c)
    landed(term_in.at[0], d_recv.at[0])
    term[2] = (bwd[facing] + term_in[0].astype(F32)).astype(BF16)
    send(term.at[2], term_in.at[2], d_send, d_recv.at[2], (r, facing))
    landed(w_z.at[pl.ds(0, 7)], r_recv.at[4])
    landed(bias_z.at[pl.ds(0, 7)], r_recv.at[5])
    normalizer = 1.0 / math.sqrt(256 * ROWS * COLS)
    w_k[k] = (total_of(w_z) * normalizer).astype(BF16)
    for step in FAR_FIRST:
        other = ahead(k, step)
        send(w_k.at[k], w_k.at[k], r_send.at[6], r_recv.at[6], at_k(other))
    grad_b[...] = total_of(bias_z) * normalizer
    landed(term_in.at[1], d_recv.at[1])
    landed(term_in.at[2], d_recv.at[2])
    source = bwd[c] + term_in[1].astype(F32) + term_in[2].astype(F32)
    grad_in[...] = lax.dot_general(
        source.astype(BF16), weight[...], (((1,), (1,)), ((), ())), preferred_element_type=F32
    ).astype(BF16)
    landed(w_k.at[pl.ds(0, 7)], r_recv.at[6])
    grad_w[...] = w_k[...].reshape(256, 256)
    landed(xg.at[pl.ds(0, 3)], a_send)
    landed(part.at[pl.ds(0, 4)], b_send)
    landed(g_all.at[pl.ds(0, 4)], c_send)
    landed(term.at[pl.ds(0, 3)], d_send)
    for i, sent in enumerate((w_out, bias_k, w_y, bias_y, w_z, bias_z, w_k)):
        landed(sent.at[pl.ds(0, 7)], r_send.at[i])


def hand_over(out, grad_in, grad_w, grad_b, out_hbm, grad_in_hbm, grad_w_hbm, grad_b_hbm, wide_w, sems):
    copies = [
        pltpu.make_async_copy(src, dst, sems.at[i])
        for i, (src, dst) in enumerate(
            ((out, out_hbm), (grad_in, grad_in_hbm), (grad_b, grad_b_hbm), (wide_w, grad_w_hbm)))
    ]
    for copy in copies[:3]:
        copy.start()
    wide_w[...] = grad_w[...].astype(F32)
    copies[3].start()
    for copy in copies:
        copy.wait()


def shards(
    features, weight, bias, block_values, block_target, block_source, block_count, cotangent
):
    vmem = pl.BlockSpec(memory_space=pltpu.VMEM)
    hbm = pl.BlockSpec(memory_space=pltpu.HBM)
    dma = pltpu.SemaphoreType.DMA
    shapes = [
        jax.ShapeDtypeStruct((256, 256), BF16),
        jax.ShapeDtypeStruct((256, 256), BF16),
        jax.ShapeDtypeStruct((256, 256), BF16),
        jax.ShapeDtypeStruct((1, 256), F32),
    ]
    results = pl.pallas_call(
        layer,
        out_shape=shapes,
        in_specs=[hbm] * 8,
        out_specs=(vmem,) * 4,
        scratch_shapes=[
            pltpu.VMEM((256, 256), BF16),
            pltpu.VMEM((1, 256), F32),
            pltpu.VMEM((256, 256), BF16),
            pltpu.VMEM((1, 1, SLOTS, BLK, BLK), BF16),
            pltpu.SMEM((1, 1, SLOTS), jnp.int32),
            pltpu.SMEM((1, 1, SLOTS), jnp.int32),
            pltpu.SMEM((1, 1), jnp.int32),
            pltpu.VMEM((2, 128), jnp.int32),
            pltpu.SMEM((2, 128), jnp.int32),
            pltpu.VMEM((SLOTS + 1, BLK, BLK), F32),
            pltpu.VMEM((SPAN * 256, COLS * 256), BF16),
            pltpu.VMEM((SPAN, 256, 256), F32),
            pltpu.VMEM((COLS, 256, 256), F32),
            pltpu.VMEM((COLS, 256, 256), BF16),
            pltpu.VMEM((COLS * 256, SPAN * 256), BF16),
            pltpu.VMEM((SPAN, 256, 256), BF16),
            pltpu.VMEM((SPAN, 256, 256), BF16),
            pltpu.VMEM((SPAN, 256, 256), BF16),
            pltpu.VMEM((COLS, 256, 256), BF16),
            pltpu.VMEM((COLS, 256, 256), BF16),
            pltpu.VMEM((8, 32, 256), F32),
            pltpu.VMEM((8, 32, 256), BF16),
            pltpu.VMEM((8, 32, 256), BF16),
            pltpu.VMEM((8, 32, 256), BF16),
            pltpu.VMEM((8, 32, 256), BF16),
            pltpu.VMEM((8, 32, 256), BF16),
            pltpu.VMEM((8, 1, 256), F32),
            pltpu.VMEM((8, 1, 256), F32),
            pltpu.VMEM((8, 1, 256), F32),
            dma((9,)),
            dma,
            dma((6,)),
            dma,
            dma((3,)),
            dma,
            dma((3,)),
            dma,
            dma((3,)),
            dma((7,)),
            dma((7,)),
            pltpu.SemaphoreType.REGULAR((2,)),
        ],
        compiler_params=pltpu.CompilerParams(
            collective_id=0, has_side_effects=True, vmem_limit_bytes=VMEM_BYTES
        ),
        name="layer",
    )(
        features, weight, bias.reshape(1, 256), block_values, block_target, block_source, block_count, cotangent
    )
    output, grad_inputs, grad_weight, grad_bias = pl.pallas_call(
        hand_over,
        out_shape=[*shapes[:2], jax.ShapeDtypeStruct((256, 256), F32), shapes[3]],
        in_specs=[vmem] * 4,
        out_specs=(hbm,) * 4,
        scratch_shapes=[pltpu.VMEM((256, 256), F32), dma((4,))],
        compiler_params=pltpu.CompilerParams(vmem_limit_bytes=1 << 20),
        name="hand_over",
    )(*results)
    return output, grad_inputs, grad_weight, grad_bias.reshape(256)


def solution(mesh):
    return jax.shard_map(
        shards,
        mesh=mesh,
        in_specs=(
            P(("row", "col"), None),
            P(),
            P(),
            P("row", "col", None, None, None),
            P("row", "col", None),
            P("row", "col", None),
            P("row", "col"),
            P(("row", "col"), None),
        ),
        out_specs=(P(("row", "col"), None), P(("row", "col"), None), P(), P()),
        check_vma=False,
    )
```

```python
import math

import jax
import jax.numpy as jnp
from jax import lax
from jax.experimental import pallas as pl
from jax.experimental.pallas import tpu as pltpu
from jax.sharding import PartitionSpec as P

BLK = 128
HALF = 2
VB = 2
SPAN = 2 * HALF + 1
COLS = 4
ROWS = 128
NY = 8
NZ = 8
SLOTS = 32
FAR_FIRST = (4, 3, 5, 2, 6, 1, 7)
VMEM_BYTES = 54810 << 10
CELLS = SPAN * VB * COLS * VB
MESH = pl.DeviceIdType.MESH
F32 = jnp.float32
BF16 = jnp.bfloat16


def dot(a, b):
    return jnp.dot(a, b, preferred_element_type=F32)


def split(value):
    high = value.astype(BF16)
    return high, (value - high.astype(F32)).astype(BF16)


def layer(
    x_hbm, weight_hbm, bias_hbm, values_hbm, target_hbm, source_hbm, count_hbm, cot_hbm,
    out, grad_in, grad_w, grad_b,
    weight, bias, cot, values, target, source_of, count, table_v, table, wide, adj, fwd, bwd,
    xg, adj_t, part, part_in, g_all, term, term_in,
    w_own, w_out, w_in, w_z, w_y, w_k, bias_k, bias_z, bias_y,
    in_sem, a_send, a_recv, b_send, b_recv, c_send, c_recv, d_send, d_recv, r_send, r_recv, ready,
):
    r = lax.axis_index("row")
    c = lax.axis_index("col")
    z = r // (2 * NY)
    xh = (r // NY) % 2
    y = r % NY
    k = xh * COLS + c
    inner = r % (2 * NY)

    def at_row(distance):
        return (lax.rem(r + distance + ROWS, ROWS), c)

    def at_col(step):
        return (r, lax.rem(c + step, COLS))

    def at_k(other):
        return (z * (2 * NY) + (other // COLS) * NY + y, lax.rem(other, COLS))

    def at_z(other):
        return (other * (2 * NY) + inner, c)

    def at_y(other):
        return (r - y + other, c)

    def ahead(me, step):
        return lax.rem(me + step, 8)

    def send(src, dst, send_sem, recv_sem, device):
        copy = pltpu.make_async_remote_copy(
            src_ref=src, dst_ref=dst, send_sem=send_sem, recv_sem=recv_sem,
            device_id=device, device_id_type=MESH,
        )
        copy.start()

    def landed(dst, sem):
        pltpu.make_async_copy(dst, dst, sem).wait()

    def total_of(parts):
        total = parts[0].astype(F32)
        for i in range(1, 8):
            total += parts[i].astype(F32)
        return total

    def local(i, src, dst):
        copy = pltpu.make_async_copy(src, dst, in_sem.at[i])
        copy.start()
        return copy

    def turn(place):
        return jnp.where(place < NY // 2, place, 3 * NY // 2 - 1 - place)

    def rank(row):
        return (4 * (row // (2 * NY)) + turn(lax.rem(row, NY))) * ROWS + row

    def signal(sem, device):
        pl.semaphore_signal(sem, inc=1, device_id=device, device_id_type=MESH)

    barrier = pltpu.get_barrier_semaphore()
    my_turn = turn(y)
    for step in range(1, COLS):
        signal(barrier, at_col(step))
    leads = []
    for distance in (1, -1):
        lead = rank(r) < rank(lax.rem(r + distance + ROWS, ROWS))
        leads.append(lead)
        pl.when(lead)(lambda distance=distance: signal(barrier, at_row(distance)))

    @pl.when(xh == 0)
    def _():
        for j in range(COLS):
            signal(barrier, at_k(COLS + j))

    @pl.loop(my_turn + 1, NY)
    def _(other):
        signal(barrier, at_y(turn(other)))

    @pl.loop(z + 1, NZ)
    def _(other):
        signal(barrier, at_z(other))

    followed = sum(jnp.where(lead, 0, 1) for lead in leads)
    scalars = [
        local(0, target_hbm, target),
        local(1, source_hbm, source_of),
        local(2, count_hbm, count),
    ]
    own_x = local(3, x_hbm, xg.at[c])
    values_in = local(4, values_hbm, values)
    late = [local(5, weight_hbm, weight), local(6, bias_hbm, bias), local(7, cot_hbm, cot)]
    pl.semaphore_wait(barrier, COLS - 1 + COLS * xh + my_turn + z + followed)
    sibling = c + 1 - 2 * lax.rem(c, 2)
    facing = lax.rem(c + 2, COLS)
    behind = lax.rem(sibling + 2, COLS)
    pieces = [pl.ds(64 * i, 64) for i in range(4)]
    for i, rows in enumerate(pieces):
        send(x_hbm.at[rows], xg.at[c, rows], a_send, a_recv.at[i], (r, facing))
    send(x_hbm.at[pieces[3]], xg.at[c, pieces[3]], a_send, a_recv.at[5], (r, behind))
    send(x_hbm, xg.at[c], a_send, a_recv.at[4], (r, sibling))
    for distance, lead in zip((1, -1), leads):
        pl.when(jnp.logical_not(lead))(lambda distance=distance: signal(ready.at[0], at_row(distance)))

    @pl.when(xh == 1)
    def _():
        for j in range(COLS):
            signal(ready.at[1], at_k(j))

    @pl.loop(0, my_turn)
    def _(other):
        signal(ready.at[1], at_y(turn(other)))

    @pl.loop(0, z)
    def _(other):
        signal(ready.at[1], at_z(other))

    for copy in scalars:
        copy.wait()
    lane = lax.broadcasted_iota(jnp.int32, (SLOTS, 128), 1)
    sub = lax.broadcasted_iota(jnp.int32, (SLOTS, 128), 0)
    in_row = jnp.full((SLOTS, 128), CELLS, jnp.int32)
    in_col = jnp.full((SLOTS, 128), CELLS, jnp.int32)
    for slot in range(SLOTS):
        cell = jnp.where(
            slot < count[0, 0], target[0, 0, slot] * (COLS * VB) + source_of[0, 0, slot], CELLS
        )
        in_row = jnp.where(lane == slot, cell, in_row)
        in_col = jnp.where(sub == slot, cell, in_col)
    table_v[0:1, :] = jnp.min(jnp.where(in_col == lane, sub, SLOTS), axis=0, keepdims=True)
    table_v[1:2, :] = jnp.min(
        jnp.where((in_col == in_row) & (sub > lane), sub, SLOTS), axis=0, keepdims=True
    )
    tabled = local(8, table_v, table)
    tabled.wait()
    values_in.wait()
    wide[SLOTS] = jnp.zeros((BLK, BLK), F32)
    for slot in range(SLOTS - 1, -1, -1):
        wide[slot] = values[0, 0, slot].astype(F32) + wide[table[1, slot]]
    for d in range(SPAN * VB):
        for e in range(COLS * VB):
            block = wide[table[0, d * (COLS * VB) + e]].astype(BF16)
            adj[d * BLK:(d + 1) * BLK, e * BLK:(e + 1) * BLK] = block
            adj_t[e * BLK:(e + 1) * BLK, d * BLK:(d + 1) * BLK] = block.T
    own_x.wait()
    landed(xg.at[sibling], a_recv.at[4])
    chip = c // 2
    near = xg[pl.ds(2 * chip, 2)].reshape(512, 256)
    near_lanes = pl.ds(pl.multiple_of(chip * 512, 512), 512)
    for offset in range(SPAN):
        fwd[offset] = dot(adj[offset * 256:(offset + 1) * 256, near_lanes], near)
    for i, rows in enumerate(pieces):
        landed(xg.at[facing, rows], a_recv.at[i])
        if i < 3:
            send(xg.at[facing, rows], xg.at[facing, rows], a_send, a_recv.at[5], (r, sibling))

    def row_block(i):
        return pl.ds(pl.multiple_of(i * 256, 256), 256)

    for offset in range(SPAN):
        fwd[offset] += dot(adj[offset * 256:(offset + 1) * 256, row_block(facing)], xg[facing])
    for copy in late:
        copy.wait()
    landed(xg.at[behind], a_recv.at[5])
    first = jnp.where(y < NY // 2, 0, 4)

    def mixed_at(offset):
        return fwd[offset] + dot(adj[row_block(offset), row_block(behind)], xg[behind])

    pl.when(followed < 2)(lambda: pl.semaphore_wait(ready.at[0], 2 - followed))
    halves = (pl.ds(0, 128), pl.ds(128, 128))
    for offset in (first, 4 - first):
        part[offset] = mixed_at(offset).astype(BF16)
        for i, rows in enumerate(halves):
            send(
                part.at[offset, rows], part_in.at[offset, rows], b_send, b_recv.at[offset // 2 + i], at_row(offset // 2 - 1))
    for offset in (1, 3, HALF):
        fwd[offset] = mixed_at(offset)
    for i, rows in enumerate(halves):
        for offset in (first, 4 - first):
            landed(part_in.at[offset, rows], b_recv.at[offset // 2 + i])
            onward = offset // 2 + 1
            part[onward, rows] = (fwd[onward, rows] + part_in[offset, rows].astype(F32)).astype(BF16)
            send(part.at[onward, rows], part_in.at[onward, rows], b_send, b_recv.at[4], at_row(offset // 2 - 1))
    landed(part_in.at[pl.ds(0, 2)], b_recv.at[4])
    mixed = fwd[HALF] + part_in[1].astype(F32) + part_in[3].astype(F32)
    high, low = split(mixed)
    pre = dot(high, weight[...]) + dot(low, weight[...]) + bias[...]
    sig = 1.0 / (1.0 + jnp.exp(-pre))
    exact = cot[...].astype(F32) * (sig * (1.0 + pre * (1.0 - sig)))
    grad = exact.astype(BF16)
    g_all[HALF] = grad
    def send_grad(src, dst, distance, arrived):
        send(g_all.at[src], g_all.at[dst], c_send, c_recv.at[arrived], at_row(distance))


    send_grad(HALF, 1, 1, 0)
    send_grad(HALF, 3, -1, 1)
    answers = COLS * (1 - xh) + (NY - 1 - my_turn) + (NZ - 1 - z)
    pl.when(answers > 0)(lambda: pl.semaphore_wait(ready.at[1], answers))
    across = (((0,), (0,)), ((), ()))
    w_term = lax.dot_general(high, grad, across, preferred_element_type=F32) + lax.dot_general(
        low, grad, across, preferred_element_type=F32
    )
    w_own[...] = w_term.reshape(8, 32, 256)
    w_out[...] = w_term.reshape(8, 32, 256).astype(BF16)
    bias_k[k] = jnp.sum(exact, axis=0, keepdims=True)
    for step in FAR_FIRST:
        other = ahead(k, step)
        send(w_out.at[other], w_in.at[k], r_send.at[0], r_recv.at[0], at_k(other))
        send(bias_k.at[k], bias_k.at[k], r_send.at[1], r_recv.at[1], at_k(other))
    w_in[k] = jnp.zeros((32, 256), BF16)
    out[...] = (pre * sig).astype(BF16)
    landed(w_in.at[pl.ds(0, 7)], r_recv.at[0])
    landed(bias_k.at[pl.ds(0, 7)], r_recv.at[1])
    w_y[y] = (w_own[k] + total_of(w_in)).astype(BF16)
    bias_y[y] = total_of(bias_k)
    for step in FAR_FIRST:
        other = ahead(y, step)
        send(w_y.at[y], w_y.at[y], r_send.at[2], r_recv.at[2], at_y(other))
        send(bias_y.at[y], bias_y.at[y], r_send.at[3], r_recv.at[3], at_y(other))
    landed(g_all.at[1], c_recv.at[0])
    send_grad(1, 0, 1, 2)
    landed(g_all.at[3], c_recv.at[1])
    send_grad(3, 4, -1, 2)
    close = g_all[pl.ds(1, 3)].reshape(768, 256)
    for j in range(COLS):
        bwd[j] = dot(adj_t[j * 256:(j + 1) * 256, 256:1024], close)
    landed(w_y.at[pl.ds(0, 7)], r_recv.at[2])
    landed(bias_y.at[pl.ds(0, 7)], r_recv.at[3])
    w_z[z] = total_of(w_y).astype(BF16)
    bias_z[z] = total_of(bias_y)
    for step in FAR_FIRST:
        other = ahead(z, step)
        send(w_z.at[z], w_z.at[z], r_send.at[4], r_recv.at[4], at_z(other))
        send(bias_z.at[z], bias_z.at[z], r_send.at[5], r_recv.at[5], at_z(other))
    landed(g_all.at[pl.ds(0, 2)], c_recv.at[2])

    def finished(j):
        rows = row_block(j)
        return bwd[j] + dot(adj_t[rows, 0:256], g_all[0]) + dot(adj_t[rows, 1024:1280], g_all[4])

    for i, other in enumerate((behind, sibling)):
        term[i] = finished(other).astype(BF16)
        send(term.at[i], term_in.at[i], d_send, d_recv.at[i], (r, sibling))
    bwd[facing] = finished(facing)
    bwd[c] = finished(c)
    landed(term_in.at[0], d_recv.at[0])
    term[2] = (bwd[facing] + term_in[0].astype(F32)).astype(BF16)
    send(term.at[2], term_in.at[2], d_send, d_recv.at[2], (r, facing))
    landed(w_z.at[pl.ds(0, 7)], r_recv.at[4])
    landed(bias_z.at[pl.ds(0, 7)], r_recv.at[5])
    normalizer = 1.0 / math.sqrt(256 * ROWS * COLS)
    w_k[k] = (total_of(w_z) * normalizer).astype(BF16)
    for step in FAR_FIRST:
        other = ahead(k, step)
        send(w_k.at[k], w_k.at[k], r_send.at[6], r_recv.at[6], at_k(other))
    grad_b[...] = total_of(bias_z) * normalizer
    landed(term_in.at[1], d_recv.at[1])
    landed(term_in.at[2], d_recv.at[2])
    source = bwd[c] + term_in[1].astype(F32) + term_in[2].astype(F32)
    grad_in[...] = lax.dot_general(
        source.astype(BF16), weight[...], (((1,), (1,)), ((), ())), preferred_element_type=F32
    ).astype(BF16)
    landed(w_k.at[pl.ds(0, 7)], r_recv.at[6])
    grad_w[...] = w_k[...].reshape(256, 256)
    landed(xg.at[pl.ds(0, 3)], a_send)
    landed(part.at[pl.ds(0, 4)], b_send)
    landed(g_all.at[pl.ds(0, 4)], c_send)
    landed(term.at[pl.ds(0, 3)], d_send)
    for i, sent in enumerate((w_out, bias_k, w_y, bias_y, w_z, bias_z, w_k)):
        landed(sent.at[pl.ds(0, 7)], r_send.at[i])


def hand_over(out, grad_in, grad_w, grad_b, out_hbm, grad_in_hbm, grad_w_hbm, grad_b_hbm, wide_w, sems):
    copies = [
        pltpu.make_async_copy(src, dst, sems.at[i])
        for i, (src, dst) in enumerate(
            ((out, out_hbm), (grad_in, grad_in_hbm), (grad_b, grad_b_hbm), (wide_w, grad_w_hbm)))
    ]
    for copy in copies[:3]:
        copy.start()
    wide_w[...] = grad_w[...].astype(F32)
    copies[3].start()
    for copy in copies:
        copy.wait()


def shards(
    features, weight, bias, block_values, block_target, block_source, block_count, cotangent
):
    vmem = pl.BlockSpec(memory_space=pltpu.VMEM)
    hbm = pl.BlockSpec(memory_space=pltpu.HBM)
    dma = pltpu.SemaphoreType.DMA
    shapes = [
        jax.ShapeDtypeStruct((256, 256), BF16),
        jax.ShapeDtypeStruct((256, 256), BF16),
        jax.ShapeDtypeStruct((256, 256), BF16),
        jax.ShapeDtypeStruct((1, 256), F32),
    ]
    results = pl.pallas_call(
        layer,
        out_shape=shapes,
        in_specs=[hbm] * 8,
        out_specs=(vmem,) * 4,
        scratch_shapes=[
            pltpu.VMEM((256, 256), BF16),
            pltpu.VMEM((1, 256), F32),
            pltpu.VMEM((256, 256), BF16),
            pltpu.VMEM((1, 1, SLOTS, BLK, BLK), BF16),
            pltpu.SMEM((1, 1, SLOTS), jnp.int32),
            pltpu.SMEM((1, 1, SLOTS), jnp.int32),
            pltpu.SMEM((1, 1), jnp.int32),
            pltpu.VMEM((2, 128), jnp.int32),
            pltpu.SMEM((2, 128), jnp.int32),
            pltpu.VMEM((SLOTS + 1, BLK, BLK), F32),
            pltpu.VMEM((SPAN * 256, COLS * 256), BF16),
            pltpu.VMEM((SPAN, 256, 256), F32),
            pltpu.VMEM((COLS, 256, 256), F32),
            pltpu.VMEM((COLS, 256, 256), BF16),
            pltpu.VMEM((COLS * 256, SPAN * 256), BF16),
            pltpu.VMEM((SPAN, 256, 256), BF16),
            pltpu.VMEM((SPAN, 256, 256), BF16),
            pltpu.VMEM((SPAN, 256, 256), BF16),
            pltpu.VMEM((COLS, 256, 256), BF16),
            pltpu.VMEM((COLS, 256, 256), BF16),
            pltpu.VMEM((8, 32, 256), F32),
            pltpu.VMEM((8, 32, 256), BF16),
            pltpu.VMEM((8, 32, 256), BF16),
            pltpu.VMEM((8, 32, 256), BF16),
            pltpu.VMEM((8, 32, 256), BF16),
            pltpu.VMEM((8, 32, 256), BF16),
            pltpu.VMEM((8, 1, 256), F32),
            pltpu.VMEM((8, 1, 256), F32),
            pltpu.VMEM((8, 1, 256), F32),
            dma((9,)),
            dma,
            dma((6,)),
            dma,
            dma((5,)),
            dma,
            dma((3,)),
            dma,
            dma((3,)),
            dma((7,)),
            dma((7,)),
            pltpu.SemaphoreType.REGULAR((2,)),
        ],
        compiler_params=pltpu.CompilerParams(
            collective_id=0, has_side_effects=True, vmem_limit_bytes=VMEM_BYTES
        ),
        name="layer",
    )(
        features, weight, bias.reshape(1, 256), block_values, block_target, block_source, block_count, cotangent
    )
    output, grad_inputs, grad_weight, grad_bias = pl.pallas_call(
        hand_over,
        out_shape=[*shapes[:2], jax.ShapeDtypeStruct((256, 256), F32), shapes[3]],
        in_specs=[vmem] * 4,
        out_specs=(hbm,) * 4,
        scratch_shapes=[pltpu.VMEM((256, 256), F32), dma((4,))],
        compiler_params=pltpu.CompilerParams(vmem_limit_bytes=1 << 20),
        name="hand_over",
    )(*results)
    return output, grad_inputs, grad_weight, grad_bias.reshape(256)


def solution(mesh):
    return jax.shard_map(
        shards,
        mesh=mesh,
        in_specs=(
            P(("row", "col"), None),
            P(),
            P(),
            P("row", "col", None, None, None),
            P("row", "col", None),
            P("row", "col", None),
            P("row", "col"),
            P(("row", "col"), None),
        ),
        out_specs=(P(("row", "col"), None), P(("row", "col"), None), P(), P()),
        check_vma=False,
    )
```
